128 devices in a mesh: cols: 2 (over core), patch: 64 (over x, y, z).
Axes of the slice: x: 4, y: 4, z: 4, core: 2. Of those that a mesh axis runs over, the one named last changes fastest.
Arguments:
- vectors: bfloat16 [262144, 512], P('patch', 'cols'), may hold values from -6 to 6
- blocks: bfloat16 [2048, 8, 128, 128], P('patch'), may hold values from -0.09375 to 0.09375
- tile_cols: int32 [2048, 8], P('patch'), may hold values from 0 to 2047, as said below
- live_tiles: int32 [64], P('patch'), may hold values from 1 to 32, as said below
Outputs:
- result: bfloat16 [262144, 512], P('patch', 'cols')
The draws below stay inside these ranges and needn't reach their ends.
Inputs may be any that keep to these rules, and one draw needn't show every extreme that they name: `tile_cols`: each listed tile lies within 4 tiles of its own tile row; entries may repeat, and repeated blocks add. `live_tiles`: some patch is full in every draw.
All inputs are finite; a program needn't handle non-finite values.
Results may differ from the reference program's by a relative error of at most 0.0064.
Values may be sent and summed in bfloat16 or wider, within the bound.
A program may use at most 128 MiB of HBM per device.

```python
import jax
import jax.numpy as jnp
from jax import lax

K = 512
TILE = 128
TILES_DEV = 32
NNZ = 8
HALO_T = 4
STEPS = 3
ITERS = 8
TILES = 2048
NV = 262144
N_PATCH = 64


def draw_tile_cols(key, part):
    first = jax.random.fold_in(key, 11)
    second = jax.random.fold_in(key, 12)
    own_ids = jnp.arange(TILES, dtype=jnp.int32)
    offsets = jax.random.randint(first, (TILES, NNZ), -HALO_T, HALO_T + 1, dtype=jnp.int32)
    signs = 2 * jax.random.randint(second, (TILES,), 0, 2, dtype=jnp.int32) - 1
    offsets = offsets.at[:, 0].set(signs * HALO_T)
    return jnp.clip(own_ids[:, None] + offsets, 0, TILES - 1).astype(jnp.int32)


def draw_live_tiles(key, part):
    first = jax.random.fold_in(key, 21)
    second = jax.random.fold_in(key, 22)
    counts = jax.random.randint(first, (N_PATCH,), 1, TILES_DEV + 1, dtype=jnp.int32)
    fullone = jax.random.randint(second, (), 0, N_PATCH, dtype=jnp.int32)
    return jnp.where(jnp.arange(N_PATCH, dtype=jnp.int32) == fullone, TILES_DEV, counts).astype(jnp.int32)


def shard_levels(key, shape, cuts, smallest, high):
    factor_of, own = 1.0, jax.random.fold_in(key, 6)
    for dim, shards_of in cuts:
        steps = jnp.exp(jax.random.uniform(jax.random.fold_in(own, dim), (shards_of,), jnp.float32, smallest / len(cuts), high / len(cuts)))
        factor_of = factor_of * jnp.repeat(steps, shape[dim] // shards_of).reshape([-1 if axis == dim else 1 for axis in range(len(shape))])
    return factor_of


def centred(own_key, shape, deviation, bound, cuts=(), held_as=jnp.bfloat16):
    drawn = jax.random.normal(own_key, shape, jnp.float32) * deviation
    if len(cuts) > 0:
        drawn = shard_levels(own_key, shape, cuts, -0.22, 0.18) * drawn
    return jnp.clip(drawn, min=-bound, max=bound).astype(held_as)


def setup_inputs(seed: int = 0) -> dict:
    splits = jax.random.split(jax.random.key(seed), 5)
    return {
        "vectors": centred(splits[0], (NV, K), 1.0, 6.0, ((0, 64), (1, 2))),
        "blocks": centred(splits[1], (TILES, NNZ, TILE, TILE), (4 * TILE * NNZ) ** -0.5, 0.09375, ((0, 64),)),
        "tile_cols": draw_tile_cols(jax.random.fold_in(splits[4], 71), 0),
        "live_tiles": draw_live_tiles(jax.random.fold_in(splits[4], 71), 0),
    }


def newton_schulz(gram):
    norm = jnp.sqrt(jnp.sum(gram * gram))
    approx = gram / norm
    identity = jnp.eye(gram.shape[0], dtype=jnp.float32)
    inverse = identity
    for sweep in range(ITERS):
        middle = 1.5 * identity - 0.5 * jnp.dot(inverse, approx, precision=lax.Precision.HIGHEST)
        approx = jnp.dot(approx, middle, precision=lax.Precision.HIGHEST)
        inverse = jnp.dot(middle, inverse, precision=lax.Precision.HIGHEST)
    return (inverse, norm)

def reference(vectors, blocks, tile_cols, live_tiles):
    tile_ids = jnp.arange(TILES, dtype=jnp.int32)
    alive = tile_ids % TILES_DEV < live_tiles[tile_ids // TILES_DEV]
    weight = alive.astype(jnp.float32)[:, None, None]
    current = (vectors.reshape(TILES, TILE, K).astype(jnp.float32) * weight).astype(jnp.bfloat16)

    def operate(field):

        def group(index):
            start = (index * TILES_DEV).astype(jnp.int32)
            listed = lax.dynamic_slice_in_dim(tile_cols, start, TILES_DEV, 0)
            stored = lax.dynamic_slice_in_dim(blocks, start, TILES_DEV, 0)
            picked = field[listed]
            return jnp.einsum('tnij,tnjc->tic', stored.astype(jnp.float32), picked.astype(jnp.float32))
        return lax.map(group, jnp.arange(N_PATCH, dtype=jnp.int32)).reshape(TILES, TILE, K)
    previous = current
    following = (weight * operate(current)).astype(jnp.bfloat16)
    for step in range(STEPS - 1):
        nextone = (weight * (2.0 * operate(following) - previous.astype(jnp.float32))).astype(jnp.bfloat16)
        previous, following = (following, nextone)
    filtered = following.reshape(NV, K)
    gram = lax.dot_general(filtered, filtered, (((0,), (0,)), ((), ())), preferred_element_type=jnp.float32)
    inverse, norm = newton_schulz(gram)
    factor = jnp.sqrt(NV / norm)
    product = jnp.dot(filtered, inverse.astype(jnp.bfloat16), preferred_element_type=jnp.float32)
    return (product * factor).astype(jnp.bfloat16)
```

```python
import functools

import jax
import jax.numpy as jnp
from jax import lax
from jax.experimental import pallas as pl
from jax.experimental.pallas import tpu as pltpu
from jax.sharding import PartitionSpec as P

MESH = pl.DeviceIdType.MESH
F32, BF16 = jnp.float32, jnp.bfloat16
TILE = 128
HALO = 4
STEPS = 3
ITERS = 8
RING = 4
SPLIT = 2


def tdot(a, b):
    return lax.dot_general(a, b, (((0,), (0,)), ((), ())), preferred_element_type=F32)


def filter_kernel(
    n_patch, cols, live, vec, blk_hbm, own_out, par_out, gram_out,
    raw, blk, ys, los, his, par, acc, pay, rsb, zb, gb,
    in_sem, blk_sem, halo_send, halo_recv, swap_send, swap_recv,
    rs_send, rs_recv, z_send, z_recv, ag_send, ag_recv, gx_send, gx_recv, out_sem,
):
    tiles, width = raw.shape[0], raw.shape[2]
    part = width // SPLIT
    core, me = lax.axis_index("cols"), lax.axis_index("patch")
    planes = n_patch // RING
    plane, z = me // RING, me % RING
    right, left = (me + 1) % n_patch, (me + n_patch - 1) % n_patch

    def plane_peer(d):
        return ((plane + d) % planes) * RING + z

    def z_peer(d):
        return plane * RING + (z + d) % RING

    def patch(index):
        return {"patch": index}

    def send(src, dst, ssem, rsem, target):
        return pltpu.make_async_remote_copy(
            src_ref=src, dst_ref=dst, send_sem=ssem, recv_sem=rsem,
            device_id=target, device_id_type=MESH,
        )

    edge = 2 * HALO
    mid = tiles - 2 * edge
    loads = [
        pltpu.make_async_copy(vec.at[pl.ds(s, n)], raw.at[pl.ds(s, n)], in_sem.at[i])
        for i, (s, n) in enumerate(((0, edge), (tiles - edge, edge), (edge, mid)))
    ]
    for copy in loads:
        copy.start()
    blk_loads = [
        pltpu.make_async_copy(blk_hbm.at[pl.ds(s, HALO)], blk.at[pl.ds(s, HALO)], blk_sem.at[i])
        for i, s in enumerate(range(0, tiles, HALO))
    ]
    for copy in blk_loads:
        copy.start()

    barrier = pltpu.get_barrier_semaphore()
    targets = [patch(right), patch(left), {"cols": 1 - core}]
    targets += [patch(plane_peer(d)) for d in range(1, planes)]
    targets += [patch(z_peer(d)) for d in range(1, RING)]
    for target in targets:
        pl.semaphore_signal(barrier, inc=1, device_id=target, device_id_type=MESH)

    def weight(t):
        return (t < live[0]).astype(F32)

    def keep(k, t, value):
        ys[k][t] = value

    def edges(k, t, slot, side):
        for h in range(SPLIT):
            side[k][h][slot] = ys[k][t, :, h * part : (h + 1) * part]

    def mask(start, count):
        def body(i, _):
            t = start + i
            ys[0][t] = (raw[t].astype(F32) * weight(t)).astype(BF16)
            return 0

        lax.fori_loop(0, count, body, 0)

    loads[0].wait()
    mask(0, edge)
    loads[1].wait()
    mask(tiles - edge, edge)

    def copy_edges(k, first, count):
        for i in range(count):
            t = first + i
            side, slot = (los, t + HALO) if t < edge else (his, t - (tiles - edge))
            edges(k, t, slot, side)

    copy_edges(0, 0, edge)
    copy_edges(0, tiles - edge, edge)
    pl.semaphore_wait(barrier, len(targets))

    def halo(k, h):
        return (
            send(
                los[k][h].at[pl.ds(HALO, HALO)], his[k][h].at[pl.ds(2 * HALO, HALO)],
                halo_send.at[k, h, 0], halo_recv.at[k, h, 0], patch(left),
            ),
            send(
                his[k][h].at[pl.ds(HALO, HALO)], los[k][h].at[pl.ds(0, HALO)],
                halo_send.at[k, h, 1], halo_recv.at[k, h, 1], patch(right),
            ),
        )

    halos = {}
    for h in range(SPLIT):
        halos[0, h] = halo(0, h)
        for copy in halos[0, h]:
            copy.start()

    loads[2].wait()
    mask(edge, mid)
    for copy in blk_loads:
        copy.wait()

    def product(k, t, source, base, lanes):
        shift = me * tiles + base
        lhs = jnp.concatenate([blk[t, n] for n in range(blk.shape[1])], axis=1)
        slots = [jnp.clip(cols[n, t] - shift, 0, source.shape[0] - 1) for n in range(blk.shape[1])]
        rhs = jnp.concatenate([source[slot] for slot in slots], axis=0)
        total = jnp.dot(lhs, rhs, preferred_element_type=F32)
        if k > 1:
            total = 2.0 * total - ys[k - 2][t, :, lanes].astype(F32)
        return (total * weight(t)).astype(BF16)

    def inner(k, start, count):
        def body(i, _):
            t = start + i
            ys[k][t] = product(k, t, ys[k - 1], 0, slice(None))
            return 0

        lax.fori_loop(0, count, body, 0)

    def outer(k, h):
        lanes = slice(h * part, (h + 1) * part)

        def low(t, _):
            value = product(k, t, los[k - 1][h], -HALO, lanes)
            ys[k][t, :, lanes] = value
            if k < STEPS:
                los[k][h][t + HALO] = value
            return 0

        def high(i, _):
            t = tiles - HALO + i
            value = product(k, t, his[k - 1][h], tiles - edge, lanes)
            ys[k][t, :, lanes] = value
            if k < STEPS:
                his[k][h][i + HALO] = value
            return 0

        halos[k - 1, h][1].wait_recv()
        lax.fori_loop(0, HALO, low, 0)
        halos[k - 1, h][0].wait_recv()
        lax.fori_loop(0, HALO, high, 0)

    swaps = []

    def swap(start, count):
        i = len(swaps)
        copy = send(
            ys[STEPS].at[pl.ds(start, count)], par.at[pl.ds(start, count)],
            swap_send.at[i], swap_recv.at[i], {"cols": 1 - core},
        )
        copy.start()
        swaps.append(copy)

    for k in range(1, STEPS + 1):
        inner(k, HALO * k, tiles - 2 * HALO * k)
    copy_edges(1, HALO, HALO)
    copy_edges(1, tiles - edge, HALO)
    swap(HALO * STEPS, tiles - 2 * HALO * STEPS)

    def gram(start, count, step):
        def body(i, _):
            rows = pl.ds(start + i * step, step)
            mine = ys[STEPS][rows].reshape(step * TILE, width)
            other = par[rows].reshape(step * TILE, width)
            acc[:, :width] += tdot(mine, mine)
            acc[:, width:] += tdot(mine, other)
            return 0

        lax.fori_loop(0, count // step, body, 0)

    acc[...] = jnp.zeros_like(acc)
    for k in range(1, STEPS + 1):
        for h in range(SPLIT):
            outer(k, h)
            if k < STEPS:
                halos[k, h] = halo(k, h)
                for copy in halos[k, h]:
                    copy.start()
        for later in range(k + 1, STEPS + 1):
            near = HALO * (later - k)
            for start in (near, tiles - HALO - near):
                inner(later, start, HALO)
                if later == k + 1 and later < STEPS:
                    copy_edges(later, start, HALO)
                if later == STEPS:
                    swap(start, HALO)
        if k == STEPS - 1:
            for copy in swaps:
                copy.wait_recv()
            gram(HALO, tiles - 2 * HALO, edge)
    early = len(swaps)
    swap(0, HALO)
    swap(tiles - HALO, HALO)
    own_copy = pltpu.make_async_copy(ys[STEPS], own_out, out_sem.at[0])
    own_copy.start()
    for copy in swaps[early:]:
        copy.wait_recv()
    par_copy = pltpu.make_async_copy(par, par_out, out_sem.at[1])
    par_copy.start()
    gram(0, HALO, HALO)
    gram(tiles - HALO, HALO, HALO)

    own = acc[:, :width]
    first = core == 0
    cross = [acc[i * TILE : (i + 1) * TILE, width:] for i in range(2)]
    chunk = pay.shape[1]
    blocks = (
        own[:TILE, :TILE],
        own[:TILE, TILE:],
        own[TILE:, TILE:],
        jnp.where(first, cross[0][:, :TILE], cross[0][:, TILE:]),
        jnp.where(first, cross[1][:, TILE:], cross[1][:, :TILE]),
    )
    flat = jnp.concatenate(blocks, axis=0).reshape(pay.shape)
    pay[...] = flat

    scatter = []
    for d in range(1, planes):
        copy = send(
            pay.at[(plane + d) % planes], rsb.at[d], rs_send.at[d], rs_recv.at[d],
            patch(plane_peer(d)),
        )
        copy.start()
        scatter.append(copy)
    total = pay[plane]
    for d in range(1, planes):
        scatter[d - 1].wait_recv()
        total = total + rsb[d]
    zb[z] = total
    along = []
    for d in range(1, RING):
        copy = send(zb.at[z], zb.at[z], z_send.at[d], z_recv.at[d], patch(z_peer(d)))
        copy.start()
        along.append(copy)
    for copy in along:
        copy.wait_recv()
    total = zb[0]
    for d in range(1, RING):
        total = total + zb[d]
    for copy in along:
        copy.wait_send()
    gb[core, plane] = total
    gather = []
    for d in range(1, planes):
        copy = send(
            gb.at[core, plane], gb.at[core, plane], ag_send.at[d], ag_recv.at[d],
            patch(plane_peer(d)),
        )
        copy.start()
        gather.append(copy)
    for copy in gather:
        copy.wait_recv()
    cross_copy = send(gb.at[core], gb.at[core], gx_send, gx_recv, {"cols": 1 - core})
    cross_copy.start()
    cross_copy.wait_recv()
    gram_copy = pltpu.make_async_copy(gb, gram_out, out_sem.at[2])
    gram_copy.start()

    for copies in halos.values():
        for copy in copies:
            copy.wait_send()
    for copy in swaps + scatter + gather + [cross_copy]:
        copy.wait_send()
    own_copy.wait()
    par_copy.wait()
    gram_copy.wait()


def filtered_and_gram(n_patch, vectors, blocks, listed, live):
    tiles, _, width = vectors.shape
    nnz = blocks.shape[1]
    planes = n_patch // RING
    chunk = 5 * TILE // planes
    part = width // SPLIT
    any_space = pl.BlockSpec(memory_space=pl.ANY)
    smem = pl.BlockSpec(memory_space=pltpu.SMEM)
    dma = pltpu.SemaphoreType.DMA
    side = [[pltpu.VMEM((3 * HALO, TILE, part), BF16) for _ in range(SPLIT)] for _ in range(STEPS)]
    swaps = 2 * STEPS + 1
    return pl.pallas_call(
        functools.partial(filter_kernel, n_patch),
        out_shape=(
            jax.ShapeDtypeStruct((tiles, TILE, width), BF16),
            jax.ShapeDtypeStruct((tiles, TILE, width), BF16),
            jax.ShapeDtypeStruct((2, planes, chunk, TILE), F32),
        ),
        in_specs=[smem, smem, any_space, any_space],
        out_specs=(any_space, any_space, any_space),
        scratch_shapes=[
            pltpu.VMEM((tiles, TILE, width), BF16),
            pltpu.VMEM((tiles, nnz, TILE, TILE), BF16),
            [pltpu.VMEM((tiles, TILE, width), BF16) for _ in range(STEPS + 1)],
            side,
            side,
            pltpu.VMEM((tiles, TILE, width), BF16),
            pltpu.VMEM((width, 2 * width), F32),
            pltpu.VMEM((planes, chunk, TILE), F32),
            pltpu.VMEM((planes, chunk, TILE), F32),
            pltpu.VMEM((RING, chunk, TILE), F32),
            pltpu.VMEM((2, planes, chunk, TILE), F32),
            dma((3,)),
            dma((tiles // HALO,)),
            dma((STEPS, SPLIT, 2)),
            dma((STEPS, SPLIT, 2)),
            dma((swaps,)),
            dma((swaps,)),
            dma((planes,)),
            dma((planes,)),
            dma((RING,)),
            dma((RING,)),
            dma((planes,)),
            dma((planes,)),
            dma,
            dma,
            dma((3,)),
        ],
        compiler_params=pltpu.CompilerParams(
            collective_id=0, has_side_effects=True, vmem_limit_bytes=60 * 2**20
        ),
        name="filter_gram",
    )(listed, live, vectors, blocks)


def rotate_kernel(
    rows_total, gram, own_hbm, par_hbm, out_hbm, full, xh, xl, zmat, zh, zl, own, par, out, in_sem, out_sem
):
    width = own.shape[2]
    size = 2 * width
    tiles = own.shape[0]
    core = lax.axis_index("cols")
    loads = [
        pltpu.make_async_copy(own_hbm, own, in_sem.at[0]),
        pltpu.make_async_copy(par_hbm, par, in_sem.at[1]),
    ]
    for copy in loads:
        copy.start()

    piece = lambda c, i: gram[c, i * TILE : (i + 1) * TILE, :]

    def put(i, j, value):
        full[i * TILE : (i + 1) * TILE, j * TILE : (j + 1) * TILE] = value
        if i != j:
            full[j * TILE : (j + 1) * TILE, i * TILE : (i + 1) * TILE] = value.T

    for c in range(2):
        put(2 * c, 2 * c, piece(c, 0))
        put(2 * c, 2 * c + 1, piece(c, 1))
        put(2 * c + 1, 2 * c + 1, piece(c, 2))
    put(0, 2, piece(0, 3))
    put(1, 3, piece(0, 4))
    put(2, 1, piece(1, 3))
    put(3, 0, piece(1, 4))

    g = full[...]
    norm = jnp.sqrt(jnp.sum(g * g))
    x = g / norm
    eye = (
        lax.broadcasted_iota(jnp.int32, (size, size), 0)
        == lax.broadcasted_iota(jnp.int32, (size, size), 1)
    ).astype(F32)
    full[...] = 1.5 * eye - 0.5 * x
    zmat[...] = full[:, pl.ds(pl.multiple_of(core * width, width), width)]

    def split(value, high, low):
        h = value.astype(BF16)
        high[...] = h
        low[...] = (value - h.astype(F32)).astype(BF16)

    full[...] = x
    split(x, xh, xl)

    def times(high, low, yh, yl):
        dot = functools.partial(jnp.dot, preferred_element_type=F32)
        return dot(high, yh) + (dot(high, yl) + dot(low, yh))

    def advance(_, carry):
        high, low = xh[...], xl[...]
        square = times(high, low, high, low)
        sh = square.astype(BF16)
        sl = (square - sh.astype(F32)).astype(BF16)
        value = 2.25 * full[...] - 1.5 * square + 0.25 * times(high, low, sh, sl)
        full[...] = value
        split(value, xh, xl)
        return carry

    def turn(_, carry):
        split(zmat[...], zh, zl)
        zmat[...] = 1.5 * zmat[...] - 0.5 * times(xh[...], xl[...], zh[...], zl[...])
        return carry

    advance(0, 0)

    def both(i, carry):
        turn(i, carry)
        return advance(i, carry)

    lax.fori_loop(1, ITERS - 1, both, 0)
    turn(0, 0)

    factor = jnp.sqrt(rows_total / norm)
    zh[...] = zmat[...].astype(BF16)
    top = zh[pl.ds(pl.multiple_of(core * width, width), width), :]
    low = zh[pl.ds(pl.multiple_of((1 - core) * width, width), width), :]
    for copy in loads:
        copy.wait()
    group = 4
    stores = []

    def rows(i, carry):
        at = pl.ds(i * group, group)
        a = own[at].reshape(group * TILE, width)
        b = par[at].reshape(group * TILE, width)
        value = jnp.dot(a, top, preferred_element_type=F32) + jnp.dot(b, low, preferred_element_type=F32)
        out[at] = (value * factor).astype(BF16).reshape(group, TILE, width)
        pltpu.make_async_copy(out.at[at], out_hbm.at[at], out_sem.at[i]).start()
        return carry

    lax.fori_loop(0, tiles // group, rows, 0)
    for i in range(tiles // group):
        at = pl.ds(i * group, group)
        pltpu.make_async_copy(out.at[at], out_hbm.at[at], out_sem.at[i]).wait()


def rotated(rows_total, gram, own, par):
    tiles, _, width = own.shape
    size = 2 * width
    any_space = pl.BlockSpec(memory_space=pl.ANY)
    vmem = pl.BlockSpec(memory_space=pltpu.VMEM)
    dma = pltpu.SemaphoreType.DMA
    return pl.pallas_call(
        functools.partial(rotate_kernel, rows_total),
        out_shape=jax.ShapeDtypeStruct(own.shape, BF16),
        in_specs=[vmem, any_space, any_space],
        out_specs=any_space,
        scratch_shapes=[
            pltpu.VMEM((size, size), F32),
            pltpu.VMEM((size, size), BF16),
            pltpu.VMEM((size, size), BF16),
            pltpu.VMEM((size, width), F32),
            pltpu.VMEM((size, width), BF16),
            pltpu.VMEM((size, width), BF16),
            pltpu.VMEM((tiles, TILE, width), BF16),
            pltpu.VMEM((tiles, TILE, width), BF16),
            pltpu.VMEM((tiles, TILE, width), BF16),
            dma((2,)),
            dma((tiles // 4,)),
        ],
        compiler_params=pltpu.CompilerParams(vmem_limit_bytes=60 * 2**20),
        name="rotate",
    )(gram, own, par)


def on_device(vectors, blocks, tile_cols, live_tiles):
    tiles, width = blocks.shape[0], vectors.shape[1]
    n_patch = lax.axis_size("patch")
    own, par, gram = filtered_and_gram(
        n_patch, vectors.reshape(tiles, TILE, width), blocks, tile_cols.T, live_tiles
    )
    result = rotated(n_patch * tiles * TILE, gram.reshape(2, -1, TILE), own, par)
    return result.reshape(tiles * TILE, width)


def solution(mesh):
    in_specs = (P("patch", "cols"), P("patch", None, None, None), P("patch", None), P("patch"))
    out_specs = P("patch", "cols")
    return jax.shard_map(
        on_device, mesh=mesh, in_specs=in_specs, out_specs=out_specs, check_vma=False
    )
```

```python
import functools

import jax
import jax.numpy as jnp
from jax import lax
from jax.experimental import pallas as pl
from jax.experimental.pallas import tpu as pltpu
from jax.sharding import PartitionSpec as P

MESH = pl.DeviceIdType.MESH
F32, BF16 = jnp.float32, jnp.bfloat16
TILE = 128
HALO = 4
STEPS = 3
ITERS = 8
RING = 4
SPLIT = 2


def tdot(a, b):
    return lax.dot_general(a, b, (((0,), (0,)), ((), ())), preferred_element_type=F32)


def filter_kernel(
    n_patch, cols, live, vec, blk_hbm, own_out, par_out, gram_out,
    raw, blk, ys, los, his, par, acc, pay, rsb, zb, gb,
    in_sem, blk_sem, halo_send, halo_recv, swap_send, swap_recv,
    rs_send, rs_recv, z_send, z_recv, ag_send, ag_recv, gx_send, gx_recv, out_sem,
):
    tiles, width = raw.shape[0], raw.shape[2]
    part = width // SPLIT
    core, me = lax.axis_index("cols"), lax.axis_index("patch")
    planes = n_patch // RING
    plane, z = me // RING, me % RING
    right, left = (me + 1) % n_patch, (me + n_patch - 1) % n_patch

    def plane_peer(d):
        return ((plane + d) % planes) * RING + z

    def z_peer(d):
        return plane * RING + (z + d) % RING

    def patch(index):
        return {"patch": index}

    def send(src, dst, ssem, rsem, target):
        return pltpu.make_async_remote_copy(
            src_ref=src, dst_ref=dst, send_sem=ssem, recv_sem=rsem,
            device_id=target, device_id_type=MESH,
        )

    edge = 2 * HALO
    mid = tiles - 2 * edge
    loads = [
        pltpu.make_async_copy(vec.at[pl.ds(s, n)], raw.at[pl.ds(s, n)], in_sem.at[i])
        for i, (s, n) in enumerate(((0, edge), (tiles - edge, edge), (edge, mid)))
    ]
    for copy in loads:
        copy.start()
    blk_loads = [
        pltpu.make_async_copy(blk_hbm.at[pl.ds(s, HALO)], blk.at[pl.ds(s, HALO)], blk_sem.at[i])
        for i, s in enumerate(range(0, tiles, HALO))
    ]
    for copy in blk_loads:
        copy.start()

    barrier = pltpu.get_barrier_semaphore()
    targets = [patch(right), patch(left), {"cols": 1 - core}]
    targets += [patch(plane_peer(d)) for d in range(1, planes)]
    targets += [patch(z_peer(d)) for d in range(1, RING)]
    for target in targets:
        pl.semaphore_signal(barrier, inc=1, device_id=target, device_id_type=MESH)

    def weight(t):
        return (t < live[0]).astype(F32)

    def keep(k, t, value):
        ys[k][t] = value

    def edges(k, t, slot, side):
        for h in range(SPLIT):
            side[k][h][slot] = ys[k][t, :, h * part : (h + 1) * part]

    def mask(start, count):
        def body(i, _):
            t = start + i
            ys[0][t] = (raw[t].astype(F32) * weight(t)).astype(BF16)
            return 0

        lax.fori_loop(0, count, body, 0)

    loads[0].wait()
    mask(0, edge)
    loads[1].wait()
    mask(tiles - edge, edge)

    def copy_edges(k, first, count):
        for i in range(count):
            t = first + i
            side, slot = (los, t + HALO) if t < edge else (his, t - (tiles - edge))
            edges(k, t, slot, side)

    copy_edges(0, 0, edge)
    copy_edges(0, tiles - edge, edge)
    pl.semaphore_wait(barrier, len(targets))

    halos = {}

    def launch(k, h, up):
        mine, theirs = (his, los) if up else (los, his)
        copy = send(
            mine[k][h].at[pl.ds(HALO, HALO)],
            theirs[k][h].at[pl.ds(0 if up else 2 * HALO, HALO)],
            halo_send.at[k, h, int(up)], halo_recv.at[k, h, int(up)], patch(right if up else left),
        )
        copy.start()
        halos[k, h, up] = copy

    for h in range(SPLIT):
        for up in (True, False):
            launch(0, h, up)

    loads[2].wait()
    mask(edge, mid)
    for copy in blk_loads:
        copy.wait()

    def product(k, t, source, base, lanes):
        shift = me * tiles + base
        lhs = jnp.concatenate([blk[t, n] for n in range(blk.shape[1])], axis=1)
        slots = [jnp.clip(cols[n, t] - shift, 0, source.shape[0] - 1) for n in range(blk.shape[1])]
        rhs = jnp.concatenate([source[slot] for slot in slots], axis=0)
        total = jnp.dot(lhs, rhs, preferred_element_type=F32)
        if k > 1:
            total = 2.0 * total - ys[k - 2][t, :, lanes].astype(F32)
        return (total * weight(t)).astype(BF16)

    def inner(k, start, count):
        def body(i, _):
            for j in range(HALO):
                t = start + i * HALO + j
                ys[k][t] = product(k, t, ys[k - 1], 0, slice(None))
            return 0

        lax.fori_loop(0, count // HALO, body, 0)

    def outer(k, h):
        lanes = slice(h * part, (h + 1) * part)
        for up in ((False, True) if k % 2 else (True, False)):
            side, slot = (his, tiles - edge) if up else (los, -HALO)
            halos[k - 1, h, not up].wait_recv()
            for i in range(HALO):
                t = tiles - HALO + i if up else i
                value = product(k, t, side[k - 1][h], slot, lanes)
                ys[k][t, :, lanes] = value
                if k < STEPS:
                    side[k][h][i + HALO] = value
            if k < STEPS:
                launch(k, h, up)

    swaps = []

    def swap(start, count):
        i = len(swaps)
        copy = send(
            ys[STEPS].at[pl.ds(start, count)], par.at[pl.ds(start, count)],
            swap_send.at[i], swap_recv.at[i], {"cols": 1 - core},
        )
        copy.start()
        swaps.append(copy)

    for k in range(1, STEPS + 1):
        inner(k, HALO * k, tiles - 2 * HALO * k)
    copy_edges(1, HALO, HALO)
    copy_edges(1, tiles - edge, HALO)
    swap(HALO * STEPS, tiles - 2 * HALO * STEPS)

    def gram(start, count, step):
        def body(i, _):
            rows = pl.ds(start + i * step, step)
            mine = ys[STEPS][rows].reshape(step * TILE, width)
            other = par[rows].reshape(step * TILE, width)
            acc[:, :width] += tdot(mine, mine)
            acc[:, width:] += tdot(mine, other)
            return 0

        lax.fori_loop(0, count // step, body, 0)

    acc[...] = jnp.zeros_like(acc)
    for k in range(1, STEPS + 1):
        for h in range(SPLIT):
            outer(k, h)
        for later in range(k + 1, STEPS + 1):
            near = HALO * (later - k)
            for start in (near, tiles - HALO - near):
                inner(later, start, HALO)
                if later == k + 1 and later < STEPS:
                    copy_edges(later, start, HALO)
                if later == STEPS:
                    swap(start, HALO)
        if k == STEPS - 1:
            for copy in swaps:
                copy.wait_recv()
            gram(HALO, tiles - 2 * HALO, edge)
    early = len(swaps)
    swap(0, HALO)
    swap(tiles - HALO, HALO)
    own_copy = pltpu.make_async_copy(ys[STEPS], own_out, out_sem.at[0])
    own_copy.start()
    for copy in swaps[early:]:
        copy.wait_recv()
    par_copy = pltpu.make_async_copy(par, par_out, out_sem.at[1])
    par_copy.start()
    gram(0, HALO, HALO)
    gram(tiles - HALO, HALO, HALO)

    own = acc[:, :width]
    first = core == 0
    cross = [acc[i * TILE : (i + 1) * TILE, width:] for i in range(2)]
    chunk = pay.shape[1]
    blocks = (
        own[:TILE, :TILE],
        own[:TILE, TILE:],
        own[TILE:, TILE:],
        jnp.where(first, cross[0][:, :TILE], cross[0][:, TILE:]),
        jnp.where(first, cross[1][:, TILE:], cross[1][:, :TILE]),
    )
    flat = jnp.concatenate(blocks, axis=0).reshape(pay.shape)
    pay[...] = flat

    scatter = []
    for d in range(1, planes):
        copy = send(
            pay.at[(plane + d) % planes], rsb.at[d], rs_send.at[d], rs_recv.at[d],
            patch(plane_peer(d)),
        )
        copy.start()
        scatter.append(copy)
    total = pay[plane]
    for d in range(1, planes):
        scatter[d - 1].wait_recv()
        total = total + rsb[d]
    zb[z] = total
    along = []
    for d in range(1, RING):
        copy = send(zb.at[z], zb.at[z], z_send.at[d], z_recv.at[d], patch(z_peer(d)))
        copy.start()
        along.append(copy)
    for copy in along:
        copy.wait_recv()
    total = zb[0]
    for d in range(1, RING):
        total = total + zb[d]
    for copy in along:
        copy.wait_send()
    gb[core, plane] = total
    gather = []
    for d in range(1, planes):
        copy = send(
            gb.at[core, plane], gb.at[core, plane], ag_send.at[d], ag_recv.at[d],
            patch(plane_peer(d)),
        )
        copy.start()
        gather.append(copy)
    across = []
    for d in range(planes):
        if d > 0:
            gather[d - 1].wait_recv()
        at = (plane + planes - d) % planes
        copy = send(gb.at[core, at], gb.at[core, at], gx_send.at[d], gx_recv.at[d], {"cols": 1 - core})
        copy.start()
        across.append(copy)
    for copy in across:
        copy.wait_recv()
    gram_copy = pltpu.make_async_copy(gb, gram_out, out_sem.at[2])
    gram_copy.start()

    for copy in list(halos.values()) + swaps + scatter + gather + across:
        copy.wait_send()
    own_copy.wait()
    par_copy.wait()
    gram_copy.wait()


def filtered_and_gram(n_patch, vectors, blocks, listed, live):
    tiles, _, width = vectors.shape
    nnz = blocks.shape[1]
    planes = n_patch // RING
    chunk = 5 * TILE // planes
    part = width // SPLIT
    any_space = pl.BlockSpec(memory_space=pl.ANY)
    smem = pl.BlockSpec(memory_space=pltpu.SMEM)
    dma = pltpu.SemaphoreType.DMA
    side = [[pltpu.VMEM((3 * HALO, TILE, part), BF16) for _ in range(SPLIT)] for _ in range(STEPS)]
    swaps = 2 * STEPS + 1
    return pl.pallas_call(
        functools.partial(filter_kernel, n_patch),
        out_shape=(
            jax.ShapeDtypeStruct((tiles, TILE, width), BF16),
            jax.ShapeDtypeStruct((tiles, TILE, width), BF16),
            jax.ShapeDtypeStruct((2, planes, chunk, TILE), F32),
        ),
        in_specs=[smem, smem, any_space, any_space],
        out_specs=(any_space, any_space, any_space),
        scratch_shapes=[
            pltpu.VMEM((tiles, TILE, width), BF16),
            pltpu.VMEM((tiles, nnz, TILE, TILE), BF16),
            [pltpu.VMEM((tiles, TILE, width), BF16) for _ in range(STEPS + 1)],
            side,
            side,
            pltpu.VMEM((tiles, TILE, width), BF16),
            pltpu.VMEM((width, 2 * width), F32),
            pltpu.VMEM((planes, chunk, TILE), F32),
            pltpu.VMEM((planes, chunk, TILE), F32),
            pltpu.VMEM((RING, chunk, TILE), F32),
            pltpu.VMEM((2, planes, chunk, TILE), F32),
            dma((3,)),
            dma((tiles // HALO,)),
            dma((STEPS, SPLIT, 2)),
            dma((STEPS, SPLIT, 2)),
            dma((swaps,)),
            dma((swaps,)),
            dma((planes,)),
            dma((planes,)),
            dma((RING,)),
            dma((RING,)),
            dma((planes,)),
            dma((planes,)),
            dma((planes,)),
            dma((planes,)),
            dma((3,)),
        ],
        compiler_params=pltpu.CompilerParams(
            collective_id=0, has_side_effects=True, vmem_limit_bytes=60 * 2**20
        ),
        name="filter_gram",
    )(listed, live, vectors, blocks)


def rotate_kernel(
    rows_total, gram, own_hbm, par_hbm, out_hbm, full, xh, xl, sh, sl, zmat, zh, zl, own, par, out, in_sem, out_sem
):
    width = own.shape[2]
    size = 2 * width
    tiles = own.shape[0]
    core = lax.axis_index("cols")
    loads = [
        pltpu.make_async_copy(own_hbm, own, in_sem.at[0]),
        pltpu.make_async_copy(par_hbm, par, in_sem.at[1]),
    ]
    for copy in loads:
        copy.start()

    piece = lambda c, i: gram[c, i * TILE : (i + 1) * TILE, :]

    def put(i, j, value):
        full[i * TILE : (i + 1) * TILE, j * TILE : (j + 1) * TILE] = value
        if i != j:
            full[j * TILE : (j + 1) * TILE, i * TILE : (i + 1) * TILE] = value.T

    for c in range(2):
        put(2 * c, 2 * c, piece(c, 0))
        put(2 * c, 2 * c + 1, piece(c, 1))
        put(2 * c + 1, 2 * c + 1, piece(c, 2))
    put(0, 2, piece(0, 3))
    put(1, 3, piece(0, 4))
    put(2, 1, piece(1, 3))
    put(3, 0, piece(1, 4))

    g = full[...]
    norm = jnp.sqrt(jnp.sum(g * g))
    x = g * (1.0 / norm)
    full[...] = x

    def split(value):
        high = value.astype(BF16)
        return high, (value - high.astype(F32)).astype(BF16)

    xh[...], xl[...] = split(x)
    start = 1.5 * (
        lax.broadcasted_iota(jnp.int32, (size, width), 0)
        == lax.broadcasted_iota(jnp.int32, (size, width), 1) + core * width
    ).astype(F32)
    z = start - 0.5 * full[:, pl.ds(pl.multiple_of(core * width, width), width)]
    zmat[...] = z
    zh[...], zl[...] = split(z)

    def times(count, ah, al, bh, bl, lanes):
        dot = functools.partial(jnp.dot, preferred_element_type=F32)
        high = ah[:count, :]
        both = dot(jnp.concatenate([high, al[:count, :]], axis=0), bh[:, lanes])
        return both[:count] + (both[count:] + dot(high, bl[:, lanes]))

    halves = [slice(i * width, (i + 1) * width) for i in range(2)]

    def keep(high, low, i, j, value):
        h, l = split(value)
        high[halves[i], halves[j]] = h
        low[halves[i], halves[j]] = l
        if i != j:
            high[halves[j], halves[i]] = h.T
            low[halves[j], halves[i]] = l.T

    upper = ((0, 0), (0, 1), (1, 1))

    def square():
        for j in (1, 0):
            s = times((j + 1) * width, xh, xl, xh, xl, halves[j])
            rows = slice(0, (j + 1) * width)
            full[rows, halves[j]] = 2.25 * full[rows, halves[j]] - 1.5 * s
            for i in range(j + 1):
                keep(sh, sl, i, j, s[halves[i]])

    def cube():
        for j in (1, 0):
            rows = slice(0, (j + 1) * width)
            p = times((j + 1) * width, xh, xl, sh, sl, halves[j])
            full[rows, halves[j]] = full[rows, halves[j]] + 0.25 * p
        for i, j in upper:
            keep(xh, xl, i, j, full[halves[i], halves[j]])

    def turn():
        zmat[...] = 1.5 * zmat[...] - 0.5 * times(size, xh, xl, zh, zl, slice(None))
        zh[...], zl[...] = split(zmat[...])

    square()
    cube()

    def both(i, carry):
        square()
        turn()
        cube()
        return carry

    lax.fori_loop(1, ITERS - 1, both, 0)
    turn()

    factor = jnp.sqrt(rows_total / norm)
    top = zh[pl.ds(pl.multiple_of(core * width, width), width), :]
    low = zh[pl.ds(pl.multiple_of((1 - core) * width, width), width), :]
    for copy in loads:
        copy.wait()
    group = 4
    stores = []

    def rows(i, carry):
        at = pl.ds(i * group, group)
        a = own[at].reshape(group * TILE, width)
        b = par[at].reshape(group * TILE, width)
        value = jnp.dot(a, top, preferred_element_type=F32) + jnp.dot(b, low, preferred_element_type=F32)
        out[at] = (value * factor).astype(BF16).reshape(group, TILE, width)
        pltpu.make_async_copy(out.at[at], out_hbm.at[at], out_sem.at[i]).start()
        return carry

    lax.fori_loop(0, tiles // group, rows, 0)
    for i in range(tiles // group):
        at = pl.ds(i * group, group)
        pltpu.make_async_copy(out.at[at], out_hbm.at[at], out_sem.at[i]).wait()


def rotated(rows_total, gram, own, par):
    tiles, _, width = own.shape
    size = 2 * width
    any_space = pl.BlockSpec(memory_space=pl.ANY)
    vmem = pl.BlockSpec(memory_space=pltpu.VMEM)
    dma = pltpu.SemaphoreType.DMA
    return pl.pallas_call(
        functools.partial(rotate_kernel, rows_total),
        out_shape=jax.ShapeDtypeStruct(own.shape, BF16),
        in_specs=[vmem, any_space, any_space],
        out_specs=any_space,
        scratch_shapes=[
            pltpu.VMEM((size, size), F32),
            pltpu.VMEM((size, size), BF16),
            pltpu.VMEM((size, size), BF16),
            pltpu.VMEM((size, size), BF16),
            pltpu.VMEM((size, size), BF16),
            pltpu.VMEM((size, width), F32),
            pltpu.VMEM((size, width), BF16),
            pltpu.VMEM((size, width), BF16),
            pltpu.VMEM((tiles, TILE, width), BF16),
            pltpu.VMEM((tiles, TILE, width), BF16),
            pltpu.VMEM((tiles, TILE, width), BF16),
            dma((2,)),
            dma((tiles // 4,)),
        ],
        compiler_params=pltpu.CompilerParams(vmem_limit_bytes=60 * 2**20),
        name="rotate",
    )(gram, own, par)


def on_device(vectors, blocks, tile_cols, live_tiles):
    tiles, width = blocks.shape[0], vectors.shape[1]
    n_patch = lax.axis_size("patch")
    own, par, gram = filtered_and_gram(
        n_patch, vectors.reshape(tiles, TILE, width), blocks, tile_cols.T, live_tiles
    )
    result = rotated(n_patch * tiles * TILE, gram.reshape(2, -1, TILE), own, par)
    return result.reshape(tiles * TILE, width)


def solution(mesh):
    in_specs = (P("patch", "cols"), P("patch", None, None, None), P("patch", None), P("patch"))
    out_specs = P("patch", "cols")
    return jax.shard_map(
        on_device, mesh=mesh, in_specs=in_specs, out_specs=out_specs, check_vma=False
    )
```

```python
import functools

import jax
import jax.numpy as jnp
from jax import lax
from jax.experimental import pallas as pl
from jax.experimental.pallas import tpu as pltpu
from jax.sharding import PartitionSpec as P

MESH = pl.DeviceIdType.MESH
F32, BF16 = jnp.float32, jnp.bfloat16
TILE = 128
HALO = 4
STEPS = 3
ITERS = 8
RING = 4
PIECES = 2
SPLIT = 2


def tdot(a, b):
    return lax.dot_general(a, b, (((0,), (0,)), ((), ())), preferred_element_type=F32)


def pack_gram(own, other, first, pay):
    row = lax.broadcasted_iota(jnp.int32, (TILE, TILE), 0)
    lane = lax.broadcasted_iota(jnp.int32, (TILE, TILE), 1)
    last = own[TILE:, TILE:]
    blocks = (
        jnp.where(row <= lane, own[:TILE, :TILE], last),
        own[:TILE, TILE:],
        jnp.where(first, other[:TILE, :TILE], other[:TILE, TILE:]),
        jnp.where(first, other[TILE:, TILE:], other[TILE:, :TILE]),
    )
    chunks = pay.shape[0]
    rows = 4 * TILE // chunks
    pay[:, :rows, :] = jnp.concatenate(blocks, axis=0).reshape(chunks, rows, TILE)
    line = jnp.sum(jnp.where(row == lane, last, 0.0), axis=0, keepdims=True)
    per = TILE // chunks
    for q in range(chunks):
        pay[q, rows:, :] = jnp.where(lane[:1] // per == q, line, 0.0)


def filter_kernel(
    n_patch, cols, live, vec, blk_hbm, own_out, par_out, gram_out,
    raw, blk, ys, los, his, par, acc, pay, rsb, zb, gb,
    in_sem, blk_sem, halo_send, halo_recv, swap_send, swap_recv,
    rs_send, rs_recv, z_send, z_recv, ag_send, ag_recv, gx_send, gx_recv, out_sem,
):
    tiles, width = raw.shape[0], raw.shape[2]
    part = width // SPLIT
    core, me = lax.axis_index("cols"), lax.axis_index("patch")
    planes = n_patch // RING
    plane, z = lax.div(me, RING), lax.rem(me, RING)
    px, py = lax.div(plane, RING), lax.rem(plane, RING)
    right, left = lax.rem(me + 1, n_patch), lax.rem(me + n_patch - 1, n_patch)

    def far(d):
        return sum(min(v, RING - v) for v in divmod(d, RING))

    offsets = sorted(range(1, planes), key=far, reverse=True)

    def plane_at(dx, dy):
        return lax.rem(px + dx, RING) * RING + lax.rem(py + dy, RING)

    peer_plane = {d: plane_at(*divmod(d, RING)) for d in offsets}
    source_plane = {d: plane_at(*((RING - v) % RING for v in divmod(d, RING))) for d in offsets}

    def plane_peer(d):
        return peer_plane[d] * RING + z

    def z_peer(d):
        return plane * RING + lax.rem(z + d, RING)

    def patch(index):
        return {"patch": index}

    def send(src, dst, ssem, rsem, target):
        return pltpu.make_async_remote_copy(
            src_ref=src, dst_ref=dst, send_sem=ssem, recv_sem=rsem,
            device_id=target, device_id_type=MESH,
        )

    edge = 2 * HALO
    mid = tiles - 2 * edge
    spans = ((0, HALO), (tiles - HALO, HALO), (HALO, HALO), (tiles - edge, HALO), (edge, mid))
    loads = [
        pltpu.make_async_copy(vec.at[pl.ds(s, n)], raw.at[pl.ds(s, n)], in_sem.at[i])
        for i, (s, n) in enumerate(spans)
    ]
    for copy in loads[:2]:
        copy.start()
    barrier = pltpu.get_barrier_semaphore()
    targets = [patch(right), patch(left), {"cols": 1 - core}]
    targets += [patch(plane_peer(d)) for d in offsets]
    targets += [patch(z_peer(d)) for d in range(1, RING)]
    for target in targets:
        pl.semaphore_signal(barrier, inc=1, device_id=target, device_id_type=MESH)
    for copy in loads[2:]:
        copy.start()
    blk_loads = [
        pltpu.make_async_copy(blk_hbm.at[pl.ds(s, HALO)], blk.at[pl.ds(s, HALO)], blk_sem.at[i])
        for i, s in enumerate(range(0, tiles, HALO))
    ]
    for copy in blk_loads[1:] + blk_loads[:1]:
        copy.start()

    def weight(t):
        return (t < live[0]).astype(F32)

    def beside(k, t, value, h, lanes):
        if t < edge:
            los[k][h][t + HALO] = value[:, lanes]
        elif t >= tiles - edge:
            his[k][h][t - (tiles - edge)] = value[:, lanes]

    lanes_of = [slice(h * part, (h + 1) * part) for h in range(SPLIT)]

    def mask(t):
        value = (raw[t].astype(F32) * weight(t)).astype(BF16)
        ys[0][t] = value
        return value

    def mask_end(start):
        for t in range(start, start + HALO):
            value = mask(t)
            for h in range(SPLIT):
                beside(0, t, value, h, lanes_of[h])

    halos = {}
    half = HALO // PIECES

    def linked(up):
        return pl.when(me != n_patch - 1) if up else pl.when(me != 0)

    @pl.when(me == 0)
    def _():
        for k in range(STEPS):
            for h in range(SPLIT):
                los[k][h][:HALO] = jnp.zeros((HALO, TILE, part), BF16)

    @pl.when(me == n_patch - 1)
    def _():
        for k in range(STEPS):
            for h in range(SPLIT):
                his[k][h][2 * HALO :] = jnp.zeros((HALO, TILE, part), BF16)

    def launch(k, h, up, p):
        mine, theirs = (his, los) if up else (los, his)
        copy = send(
            mine[k][h].at[pl.ds(HALO + p * half, half)],
            theirs[k][h].at[pl.ds((0 if up else 2 * HALO) + p * half, half)],
            halo_send.at[k, h, int(up), p], halo_recv.at[k, h, int(up), p], patch(right if up else left),
        )
        linked(up)(copy.start)
        halos[k, h, up, p] = copy

    loads[0].wait()
    mask_end(0)
    loads[1].wait()
    mask_end(tiles - HALO)
    pl.semaphore_wait(barrier, len(targets))
    for h in range(SPLIT):
        for up in (True, False):
            for p in range(PIECES):
                launch(0, h, up, p)
    loads[2].wait()
    mask_end(HALO)
    loads[3].wait()
    mask_end(tiles - edge)
    loads[4].wait()

    def mask_mid(i, _):
        for j in range(HALO):
            mask(edge + i * HALO + j)
        return 0

    lax.fori_loop(0, mid // HALO, mask_mid, 0)

    def product(k, t, source, base, lanes):
        shift = me * tiles + base
        lhs = jnp.concatenate([blk[t, n] for n in range(blk.shape[1])], axis=1)
        slots = [jnp.clip(cols[n, t] - shift, 0, source.shape[0] - 1) for n in range(blk.shape[1])]
        rhs = jnp.concatenate([source[slot] for slot in slots], axis=0)
        total = jnp.dot(lhs, rhs, preferred_element_type=F32)
        if k > 1:
            total = 2.0 * total - ys[k - 2][t, :, lanes].astype(F32)
        return (total * weight(t)).astype(BF16)

    def inner(k, start, count, loading=False):
        def body(i, _):
            first = start + i * HALO
            if loading:
                rows = pl.ds(first, HALO)
                pltpu.make_async_copy(blk_hbm.at[rows], blk.at[rows], blk_sem.at[lax.div(first, HALO)]).wait()
            for j in range(HALO):
                t = first + j
                ys[k][t] = product(k, t, ys[k - 1], 0, slice(None))
            return 0

        lax.fori_loop(0, count // HALO, body, 0)

    swaps = []

    def swap(start, count, lanes):
        i = len(swaps)
        copy = send(
            ys[STEPS].at[pl.ds(start, count), :, lanes], par.at[pl.ds(start, count), :, lanes],
            swap_send.at[i], swap_recv.at[i], {"cols": 1 - core},
        )
        copy.start()
        swaps.append(copy)

    every = slice(0, width)

    def copy_ends(k, first):
        for t in range(first, first + HALO):
            for h in range(SPLIT):
                beside(k, t, ys[k][t], h, lanes_of[h])

    def outer(k, h):
        for up in ((False, True) if k % 2 else (True, False)):
            side, slot = (his, tiles - edge) if up else (los, -HALO)
            first = tiles - HALO if up else 0
            for p in range(PIECES):
                linked(up)(halos[k - 1, h, not up, p].wait_recv)
            for p in range(PIECES):
                for t in range(first + p * half, first + (p + 1) * half):
                    value = product(k, t, side[k - 1][h], slot, lanes_of[h])
                    ys[k][t, :, lanes_of[h]] = value
                    if k < STEPS:
                        beside(k, t, value, h, slice(None))
                if k < STEPS:
                    launch(k, h, up, p)
            if k == STEPS:
                swap(first, HALO, lanes_of[h])

    inner(1, HALO, tiles - 2 * HALO, loading=True)
    for copy in (blk_loads[0], blk_loads[-1]):
        copy.wait()
    copy_ends(1, HALO)
    copy_ends(1, tiles - edge)
    inner(2, 2 * HALO, tiles - 4 * HALO)

    def gram(start, count, step):
        def body(i, _):
            rows = pl.ds(start + i * step, step)
            mine = ys[STEPS][rows].reshape(step * TILE, width)
            other = par[rows].reshape(step * TILE, width)
            acc[:, :width] += tdot(mine, mine)
            acc[:, width:] += tdot(mine, other)
            return 0

        lax.fori_loop(0, count // step, body, 0)

    acc[...] = jnp.zeros_like(acc)
    for k in range(1, STEPS + 1):
        for h in range(SPLIT):
            outer(k, h)
        if k == 1:
            inner(STEPS, HALO * STEPS, tiles - 2 * HALO * STEPS)
            swap(HALO * STEPS, tiles - 2 * HALO * STEPS, every)
        for later in range(k + 1, STEPS + 1):
            near = HALO * (later - k)
            for start in (near, tiles - HALO - near):
                inner(later, start, HALO)
                if later == k + 1 and later < STEPS:
                    copy_ends(later, start)
                if later == STEPS:
                    swap(start, HALO, every)
        if k == STEPS - 1:
            early = len(swaps)
            for copy in swaps:
                copy.wait_recv()
            gram(HALO, tiles - 2 * HALO, edge)
    own_copy = pltpu.make_async_copy(ys[STEPS], own_out, out_sem.at[0])
    own_copy.start()

    def ends(ref):
        rows = [ref[pl.ds(s, HALO)].reshape(HALO * TILE, width) for s in (0, tiles - HALO)]
        return jnp.concatenate(rows, axis=0)

    mine = ends(ys[STEPS])
    acc[:, :width] += tdot(mine, mine)
    for copy in swaps[early:]:
        copy.wait_recv()
    par_copy = pltpu.make_async_copy(par, par_out, out_sem.at[1])
    par_copy.start()
    acc[:, width:] += tdot(ends(ys[STEPS]), ends(par))
    pack_gram(acc[:, :width], acc[:, width:], core == 0, pay)

    scatter = []
    for d in offsets:
        copy = send(pay.at[peer_plane[d]], rsb.at[d], rs_send.at[d], rs_recv.at[d], patch(plane_peer(d)))
        copy.start()
        scatter.append(copy)
    total = pay[plane]
    for d, copy in zip(offsets[::-1], scatter[::-1]):
        copy.wait_recv()
        total = total + rsb[d]
    zb[z] = total
    along = []
    for d in range(1, RING):
        copy = send(zb.at[z], zb.at[z], z_send.at[d], z_recv.at[d], patch(z_peer(d)))
        copy.start()
        along.append(copy)
    for copy in along:
        copy.wait_recv()
    total = zb[0]
    for d in range(1, RING):
        total = total + zb[d]
    for copy in along:
        copy.wait_send()
    gb[core, plane] = total
    gather = []
    for d in offsets:
        copy = send(
            gb.at[core, plane], gb.at[core, plane], ag_send.at[d], ag_recv.at[d], patch(plane_peer(d))
        )
        copy.start()
        gather.append(copy)
    across = []

    def cross(d, at):
        copy = send(gb.at[core, at], gb.at[core, at], gx_send.at[d], gx_recv.at[d], {"cols": 1 - core})
        copy.start()
        across.append(copy)

    cross(0, plane)
    for d, copy in zip(offsets[::-1], gather[::-1]):
        copy.wait_recv()
        cross(d, source_plane[d])
    for copy in across:
        copy.wait_recv()
    gram_copy = pltpu.make_async_copy(gb, gram_out, out_sem.at[2])
    gram_copy.start()

    for (k, h, up, p), copy in halos.items():
        linked(up)(copy.wait_send)
    for copy in swaps + scatter + gather + across:
        copy.wait_send()
    own_copy.wait()
    par_copy.wait()
    gram_copy.wait()


def filtered_and_gram(n_patch, vectors, blocks, listed, live):
    tiles, _, width = vectors.shape
    nnz = blocks.shape[1]
    planes = n_patch // RING
    chunk = 4 * TILE // planes + 1
    part = width // SPLIT
    any_space = pl.BlockSpec(memory_space=pl.ANY)
    hbm = pl.BlockSpec(memory_space=pltpu.HBM)
    smem = pl.BlockSpec(memory_space=pltpu.SMEM)
    dma = pltpu.SemaphoreType.DMA
    side = [[pltpu.VMEM((3 * HALO, TILE, part), BF16) for _ in range(SPLIT)] for _ in range(STEPS)]
    swaps = 2 * STEPS - 1 + 2 * SPLIT
    return pl.pallas_call(
        functools.partial(filter_kernel, n_patch),
        out_shape=(
            jax.ShapeDtypeStruct((tiles, TILE, width), BF16),
            jax.ShapeDtypeStruct((tiles, TILE, width), BF16),
            jax.ShapeDtypeStruct((2, planes, chunk, TILE), F32),
        ),
        in_specs=[smem, smem, hbm, hbm],
        out_specs=(any_space, any_space, any_space),
        scratch_shapes=[
            pltpu.VMEM((tiles, TILE, width), BF16),
            pltpu.VMEM((tiles, nnz, TILE, TILE), BF16),
            [pltpu.VMEM((tiles, TILE, width), BF16) for _ in range(STEPS + 1)],
            side,
            side,
            pltpu.VMEM((tiles, TILE, width), BF16),
            pltpu.VMEM((width, 2 * width), F32),
            pltpu.VMEM((planes, chunk, TILE), F32),
            pltpu.VMEM((planes, chunk, TILE), F32),
            pltpu.VMEM((RING, chunk, TILE), F32),
            pltpu.VMEM((2, planes, chunk, TILE), F32),
            dma((5,)),
            dma((tiles // HALO,)),
            dma((STEPS, SPLIT, 2, PIECES)),
            dma((STEPS, SPLIT, 2, PIECES)),
            dma((swaps,)),
            dma((swaps,)),
            dma((planes,)),
            dma((planes,)),
            dma((RING,)),
            dma((RING,)),
            dma((planes,)),
            dma((planes,)),
            dma((planes,)),
            dma((planes,)),
            dma((3,)),
        ],
        compiler_params=pltpu.CompilerParams(
            collective_id=0, has_side_effects=True, vmem_limit_bytes=48 * 2**20
        ),
        name="filter_gram",
    )(listed, live, vectors, blocks)


def rotate_kernel(
    rows_total, gram, own_hbm, par_hbm, out_hbm, full, xh, xl, sh, sl, zmat, zh, zl, own, par, out, in_sem, out_sem
):
    width = own.shape[2]
    size = 2 * width
    tiles = own.shape[0]
    core = lax.axis_index("cols")
    loads = [
        pltpu.make_async_copy(own_hbm, own, in_sem.at[0]),
        pltpu.make_async_copy(par_hbm, par, in_sem.at[1]),
    ]
    for copy in loads:
        copy.start()

    row = lax.broadcasted_iota(jnp.int32, (TILE, TILE), 0)
    lane = lax.broadcasted_iota(jnp.int32, (TILE, TILE), 1)
    per = gram.shape[1] // 4

    def piece(c, i):
        return gram[c, i * per : (i + 1) * per, : TILE // per, :].reshape(TILE, TILE)

    blocks = {}
    for c in range(2):
        mixed, line = piece(c, 0), jnp.sum(gram[c, :, TILE // per :, :], axis=0)
        turned = mixed.T
        blocks[2 * c, 2 * c] = jnp.where(row <= lane, mixed, turned)
        blocks[2 * c + 1, 2 * c + 1] = jnp.where(row > lane, mixed, jnp.where(row < lane, turned, line))
        blocks[2 * c, 2 * c + 1] = piece(c, 1)
    blocks[0, 2], blocks[1, 3] = piece(0, 2), piece(0, 3)
    blocks[2, 1], blocks[3, 0] = piece(1, 2), piece(1, 3)
    total = sum((1.0 if i == j else 2.0) * jnp.sum(v * v, axis=0, keepdims=True) for (i, j), v in blocks.items())
    norm = jnp.sqrt(jnp.sum(total))
    inv = 1.0 / norm

    def put(i, j, value):
        full[i * TILE : (i + 1) * TILE, j * TILE : (j + 1) * TILE] = value

    for (i, j), value in blocks.items():
        value = value * inv
        if i <= j:
            put(i, j, value)
        if i > j or (i, j) in ((0, 1), (2, 3)):
            put(j, i, value.T)

    def split(value):
        high = value.astype(BF16)
        return high, (value - high.astype(F32)).astype(BF16)

    halves = [slice(i * width, (i + 1) * width) for i in range(2)]
    upper = ((0, 0), (0, 1), (1, 1))

    def keep(high, low, i, j, value):
        h, l = split(value)
        high[halves[i], halves[j]] = h
        low[halves[i], halves[j]] = l
        if i != j:
            high[halves[j], halves[i]] = h.T
            low[halves[j], halves[i]] = l.T

    for i, j in upper:
        keep(xh, xl, i, j, full[halves[i], halves[j]])
    mine = pl.ds(pl.multiple_of(core * width, width), width)
    eye = (
        lax.broadcasted_iota(jnp.int32, (size, width), 0)
        == lax.broadcasted_iota(jnp.int32, (size, width), 1) + core * width
    )
    z = jnp.where(eye, 1.5, 0.0) - 0.5 * (xh[:, mine].astype(F32) + xl[:, mine].astype(F32))
    zmat[...] = z
    zh[...], zl[...] = split(z)

    def times(count, ah, al, bh, bl, lanes):
        dot = functools.partial(jnp.dot, preferred_element_type=F32)
        high = ah[:count, :]
        both = dot(jnp.concatenate([high, al[:count, :]], axis=0), bh[:, lanes])
        return both[:count] + (both[count:] + dot(high, bl[:, lanes]))

    def square():
        for j in (1, 0):
            s = times((j + 1) * width, xh, xl, xh, xl, halves[j])
            rows = slice(0, (j + 1) * width)
            full[rows, halves[j]] = 2.25 * full[rows, halves[j]] - 1.5 * s
            for i in range(j + 1):
                keep(sh, sl, i, j, s[halves[i]])

    def cube():
        for j in (1, 0):
            rows = slice(0, (j + 1) * width)
            p = times((j + 1) * width, xh, xl, sh, sl, halves[j])
            full[rows, halves[j]] = full[rows, halves[j]] + 0.25 * p
        for i, j in upper:
            keep(xh, xl, i, j, full[halves[i], halves[j]])

    def turn():
        zmat[...] = 1.5 * zmat[...] - 0.5 * times(size, xh, xl, zh, zl, slice(None))
        zh[...], zl[...] = split(zmat[...])

    square()
    cube()

    def both(i, carry):
        square()
        turn()
        cube()
        return carry

    lax.fori_loop(1, ITERS - 1, both, 0)
    turn()

    factor = jnp.sqrt(rows_total / norm)
    top = zh[pl.ds(pl.multiple_of(core * width, width), width), :]
    low = zh[pl.ds(pl.multiple_of((1 - core) * width, width), width), :]
    zl[...] = jnp.concatenate([top, low], axis=0)
    for copy in loads:
        copy.wait()
    group = 4
    stores = []
    for i in range(tiles // group):
        at = pl.ds(i * group, group)
        a = own[at].reshape(group * TILE, width)
        b = par[at].reshape(group * TILE, width)
        value = jnp.dot(jnp.concatenate([a, b], axis=1), zl[...], preferred_element_type=F32)
        out[at] = (value * factor).astype(BF16).reshape(group, TILE, width)
        stores.append(pltpu.make_async_copy(out.at[at], out_hbm.at[at], out_sem.at[i]))
        stores[-1].start()
    for copy in stores:
        copy.wait()


def rotated(rows_total, gram, own, par):
    tiles, _, width = own.shape
    size = 2 * width
    any_space = pl.BlockSpec(memory_space=pl.ANY)
    vmem = pl.BlockSpec(memory_space=pltpu.VMEM)
    dma = pltpu.SemaphoreType.DMA
    return pl.pallas_call(
        functools.partial(rotate_kernel, rows_total),
        out_shape=jax.ShapeDtypeStruct(own.shape, BF16),
        in_specs=[vmem, any_space, any_space],
        out_specs=any_space,
        scratch_shapes=[
            pltpu.VMEM((size, size), F32),
            pltpu.VMEM((size, size), BF16),
            pltpu.VMEM((size, size), BF16),
            pltpu.VMEM((size, size), BF16),
            pltpu.VMEM((size, size), BF16),
            pltpu.VMEM((size, width), F32),
            pltpu.VMEM((size, width), BF16),
            pltpu.VMEM((size, width), BF16),
            pltpu.VMEM((tiles, TILE, width), BF16),
            pltpu.VMEM((tiles, TILE, width), BF16),
            pltpu.VMEM((tiles, TILE, width), BF16),
            dma((2,)),
            dma((tiles // 4,)),
        ],
        compiler_params=pltpu.CompilerParams(vmem_limit_bytes=48 * 2**20),
        name="rotate",
    )(gram, own, par)


def on_device(vectors, blocks, tile_cols, live_tiles):
    tiles, width = blocks.shape[0], vectors.shape[1]
    n_patch = lax.axis_size("patch")
    own, par, gram = filtered_and_gram(
        n_patch, vectors.reshape(tiles, TILE, width), blocks, tile_cols.T, live_tiles
    )
    result = rotated(n_patch * tiles * TILE, gram, own, par)
    return result.reshape(tiles * TILE, width)


def solution(mesh):
    in_specs = (P("patch", "cols"), P("patch", None, None, None), P("patch", None), P("patch"))
    out_specs = P("patch", "cols")
    return jax.shard_map(
        on_device, mesh=mesh, in_specs=in_specs, out_specs=out_specs, check_vma=False
    )
```

```python
import functools

import jax
import jax.numpy as jnp
from jax import lax
from jax.experimental import pallas as pl
from jax.experimental.pallas import tpu as pltpu
from jax.sharding import PartitionSpec as P

MESH = pl.DeviceIdType.MESH
F32, BF16 = jnp.float32, jnp.bfloat16
TILE = 128
HALO = 4
STEPS = 3
ITERS = 8
RING = 4
GROUP = 4
PIECES = 2
SPLIT = 2


def tdot(a, b):
    return lax.dot_general(a, b, (((0,), (0,)), ((), ())), preferred_element_type=F32)


def pack_gram(own, other, first, pay):
    row = lax.broadcasted_iota(jnp.int32, (TILE, TILE), 0)
    lane = lax.broadcasted_iota(jnp.int32, (TILE, TILE), 1)
    last = own[TILE:, TILE:]
    blocks = (
        jnp.where(row <= lane, own[:TILE, :TILE], last),
        own[:TILE, TILE:],
        jnp.where(first, other[:TILE, :TILE], other[:TILE, TILE:]),
        jnp.where(first, other[TILE:, TILE:], other[TILE:, :TILE]),
    )
    chunks = pay.shape[0]
    rows = 4 * TILE // chunks
    pay[:, :rows, :] = jnp.concatenate(blocks, axis=0).reshape(chunks, rows, TILE)
    line = jnp.sum(jnp.where(row == lane, last, 0.0), axis=0, keepdims=True)
    per = TILE // chunks
    for q in range(chunks):
        pay[q, rows:, :] = jnp.where(lane[:1] // per == q, line, 0.0)


def filter_kernel(
    n_patch, cols_hbm, live, vec, blk_hbm, own_out, par_out, gram_out,
    cols, raw, blk, ys, los, his, par, acc, pay, rsb, zb, tot,
    in_sem, blk_sem, halo_send, halo_recv, core_send, core_recv, swap_recv,
    plane_send, rs_recv, ag_recv, z_send, z_recv,
):
    tiles, width = raw.shape[0], raw.shape[2]
    part = width // SPLIT
    core, me = lax.axis_index("cols"), lax.axis_index("patch")
    planes = n_patch // RING
    plane, z = lax.div(me, RING), lax.rem(me, RING)
    px, py = lax.div(plane, RING), lax.rem(plane, RING)
    right, left = lax.rem(me + 1, n_patch), lax.rem(me + n_patch - 1, n_patch)

    def far(d):
        return sum(min(v, RING - v) for v in divmod(d, RING))

    offsets = sorted(range(1, planes), key=far, reverse=True)

    def plane_at(dx, dy):
        return lax.rem(px + dx, RING) * RING + lax.rem(py + dy, RING)

    peer_plane = {d: plane_at(*divmod(d, RING)) for d in offsets}
    source_plane = {d: plane_at(*((RING - v) % RING for v in divmod(d, RING))) for d in offsets}

    def plane_peer(d):
        return peer_plane[d] * RING + z

    def z_peer(d):
        return plane * RING + lax.rem(z + d, RING)

    def patch(index):
        return {"patch": index}

    def send(src, dst, ssem, rsem, target):
        return pltpu.make_async_remote_copy(
            src_ref=src, dst_ref=dst, send_sem=ssem, recv_sem=rsem,
            device_id=target, device_id_type=MESH,
        )

    edge = 2 * HALO
    mid = tiles - 2 * edge
    spans = ((0, HALO), (tiles - HALO, HALO), (HALO, HALO), (tiles - edge, HALO), (edge, mid))
    loads = [
        pltpu.make_async_copy(vec.at[pl.ds(s, n)], raw.at[pl.ds(s, n)], in_sem.at[i])
        for i, (s, n) in enumerate(spans)
    ]
    for copy in loads[:2]:
        copy.start()
    barrier = pltpu.get_barrier_semaphore()
    targets = [patch(right), patch(left), {"cols": 1 - core}]
    targets += [patch(plane_peer(d)) for d in offsets]
    targets += [patch(z_peer(d)) for d in range(1, RING)]
    for target in targets:
        pl.semaphore_signal(barrier, inc=1, device_id=target, device_id_type=MESH)
    list_load = pltpu.make_async_copy(cols_hbm, cols, in_sem.at[5])
    list_load.start()
    for copy in loads[2:]:
        copy.start()
    blk_loads = [
        pltpu.make_async_copy(blk_hbm.at[pl.ds(s, HALO)], blk.at[pl.ds(s, HALO)], blk_sem.at[i])
        for i, s in enumerate(range(0, tiles, HALO))
    ]
    for copy in blk_loads[1:] + blk_loads[:1]:
        copy.start()

    def weight(t):
        return (t < live[0]).astype(F32)

    def beside(k, t, value, h, lanes):
        if t < edge:
            los[k][h][t + HALO] = value[:, lanes]
        elif t >= tiles - edge:
            his[k][h][t - (tiles - edge)] = value[:, lanes]

    lanes_of = [slice(h * part, (h + 1) * part) for h in range(SPLIT)]

    def mask(t):
        value = (raw[t].astype(F32) * weight(t)).astype(BF16)
        ys[0][t] = value
        return value

    def mask_end(start):
        for t in range(start, start + HALO):
            value = mask(t)
            for h in range(SPLIT):
                beside(0, t, value, h, lanes_of[h])

    halos = {}
    half = HALO // PIECES

    def linked(up):
        return pl.when(me != n_patch - 1) if up else pl.when(me != 0)

    @pl.when(me == 0)
    def _():
        for k in range(STEPS):
            for h in range(SPLIT):
                los[k][h][:HALO] = jnp.zeros((HALO, TILE, part), BF16)

    @pl.when(me == n_patch - 1)
    def _():
        for k in range(STEPS):
            for h in range(SPLIT):
                his[k][h][2 * HALO :] = jnp.zeros((HALO, TILE, part), BF16)

    def launch(k, h, up, p):
        mine, theirs = (his, los) if up else (los, his)
        copy = send(
            mine[k][h].at[pl.ds(HALO + p * half, half)],
            theirs[k][h].at[pl.ds((0 if up else 2 * HALO) + p * half, half)],
            halo_send.at[h, int(up), p], halo_recv.at[k % 2, h, int(up), p], patch(right if up else left),
        )
        if k > 0:
            linked(up)(halos[k - 1, h, up, p].wait_send)
        linked(up)(copy.start)
        halos[k, h, up, p] = copy

    loads[0].wait()
    mask_end(0)
    loads[1].wait()
    mask_end(tiles - HALO)
    pl.semaphore_wait(barrier, len(targets))
    for h in range(SPLIT):
        for up in (True, False):
            for p in range(PIECES):
                launch(0, h, up, p)
    loads[2].wait()
    mask_end(HALO)
    loads[3].wait()
    mask_end(tiles - edge)
    loads[4].wait()

    def mask_mid(i, _):
        for j in range(HALO):
            mask(edge + i * HALO + j)
        return 0

    lax.fori_loop(0, mid // HALO, mask_mid, 0)

    def product(k, t, source, base, lanes):
        shift = me * tiles + base
        lhs = jnp.concatenate([blk[t, n] for n in range(blk.shape[1])], axis=1)
        slots = [jnp.clip(cols[n, t] - shift, 0, source.shape[0] - 1) for n in range(blk.shape[1])]
        rhs = jnp.concatenate([source[slot] for slot in slots], axis=0)
        total = jnp.dot(lhs, rhs, preferred_element_type=F32)
        if k > 1:
            total = 2.0 * total - ys[k - 2][t, :, lanes].astype(F32)
        return (total * weight(t)).astype(BF16)

    def inner(k, start, count, loading=False):
        def body(i, _):
            first = start + i * HALO
            if loading:
                rows = pl.ds(first, HALO)
                pltpu.make_async_copy(blk_hbm.at[rows], blk.at[rows], blk_sem.at[lax.div(first, HALO)]).wait()
            for j in range(HALO):
                t = first + j
                ys[k][t] = product(k, t, ys[k - 1], 0, slice(None))
            return 0

        lax.fori_loop(0, count // HALO, body, 0)

    swaps = []

    def swap(start, count, lanes):
        i = len(swaps)
        copy = send(
            ys[STEPS].at[pl.ds(start, count), :, lanes], par.at[pl.ds(start, count), :, lanes],
            core_send.at[i], swap_recv.at[i], {"cols": 1 - core},
        )
        copy.start()
        swaps.append(copy)

    every = slice(0, width)

    def copy_ends(k, first):
        for t in range(first, first + HALO):
            for h in range(SPLIT):
                beside(k, t, ys[k][t], h, lanes_of[h])

    def outer(k, h):
        for up in ((False, True) if k % 2 else (True, False)):
            side, slot = (his, tiles - edge) if up else (los, -HALO)
            first = tiles - HALO if up else 0
            for p in range(PIECES):
                linked(up)(halos[k - 1, h, not up, p].wait_recv)
            for p in range(PIECES):
                for t in range(first + p * half, first + (p + 1) * half):
                    value = product(k, t, side[k - 1][h], slot, lanes_of[h])
                    ys[k][t, :, lanes_of[h]] = value
                    if k < STEPS:
                        beside(k, t, value, h, slice(None))
                if k < STEPS:
                    launch(k, h, up, p)
            if k == STEPS:
                swap(first, HALO, lanes_of[h])

    list_load.wait()
    inner(1, HALO, tiles - 2 * HALO, loading=True)
    for copy in (blk_loads[0], blk_loads[-1]):
        copy.wait()
    copy_ends(1, HALO)
    copy_ends(1, tiles - edge)
    inner(2, 2 * HALO, tiles - 4 * HALO)

    def gram(start, count, step):
        def body(i, _):
            rows = pl.ds(start + i * step, step)
            mine = ys[STEPS][rows].reshape(step * TILE, width)
            other = par[rows].reshape(step * TILE, width)
            acc[:, :width] += tdot(mine, mine)
            acc[:, width:] += tdot(mine, other)
            return 0

        lax.fori_loop(0, count // step, body, 0)

    acc[...] = jnp.zeros_like(acc)
    for k in range(1, STEPS + 1):
        for h in range(SPLIT):
            outer(k, h)
        if k == 1:
            for start in (HALO, tiles - edge):
                inner(2, start, HALO)
                copy_ends(2, start)
            inner(STEPS, HALO * STEPS, tiles - 2 * HALO * STEPS)
            swap(HALO * STEPS, tiles - 2 * HALO * STEPS, every)
        if k == 2:
            for start in (2 * HALO, tiles - 3 * HALO, HALO, tiles - edge):
                inner(STEPS, start, HALO)
                swap(start, HALO, every)
        if k == STEPS - 1:
            early = len(swaps)
            for copy in swaps:
                copy.wait_recv()
            gram(HALO, tiles - 2 * HALO, edge)
    own_copy = pltpu.make_async_copy(ys[STEPS], own_out, in_sem.at[0])
    own_copy.start()

    def ends(ref):
        rows = [ref[pl.ds(s, HALO)].reshape(HALO * TILE, width) for s in (0, tiles - HALO)]
        return jnp.concatenate(rows, axis=0)

    mine = ends(ys[STEPS])
    acc[:, :width] += tdot(mine, mine)
    for copy in swaps[early:]:
        copy.wait_recv()
    par_copy = pltpu.make_async_copy(par, par_out, in_sem.at[1])
    par_copy.start()
    acc[:, width:] += tdot(ends(ys[STEPS]), ends(par))
    pack_gram(acc[:, :width], acc[:, width:], core == 0, pay)

    scatter = []
    for d in offsets:
        copy = send(pay.at[peer_plane[d]], rsb.at[d], plane_send.at[d - 1], rs_recv.at[d - 1], patch(plane_peer(d)))
        copy.start()
        scatter.append(copy)
    total = pay[plane]
    for d, copy in zip(offsets[::-1], scatter[::-1]):
        copy.wait_recv()
        total = total + rsb[d]
    zb[z] = total
    along = []
    for d in range(1, RING):
        copy = send(zb.at[z], zb.at[z], z_send.at[d - 1], z_recv.at[d - 1], patch(z_peer(d)))
        copy.start()
        along.append(copy)
    for (k, h, up, p), copy in halos.items():
        if k == STEPS - 1:
            linked(up)(copy.wait_send)
    for copy in swaps + scatter:
        copy.wait_send()
    own_copy.wait()
    par_copy.wait()
    for copy in along:
        copy.wait_recv()
    total = zb[0]
    for d in range(1, RING):
        total = total + zb[d]
    for copy in along:
        copy.wait_send()
    tot[...] = total
    gather = []
    for d in offsets:
        copy = send(tot, gram_out.at[core, plane], plane_send.at[d - 1], ag_recv.at[d - 1], patch(plane_peer(d)))
        copy.start()
        gather.append(copy)
    across = []

    def cross(d, src, at):
        copy = send(src, gram_out.at[core, at], core_send.at[d], core_recv.at[d], {"cols": 1 - core})
        copy.start()
        across.append(copy)

    cross(0, tot, plane)
    gram_copy = pltpu.make_async_copy(tot, gram_out.at[core, plane], in_sem.at[2])
    gram_copy.start()
    for d, copy in zip(offsets[::-1], gather[::-1]):
        copy.wait_recv()
        cross(d, gram_out.at[core, source_plane[d]], source_plane[d])
    for copy in across:
        copy.wait_recv()
    for copy in gather + across:
        copy.wait_send()
    gram_copy.wait()


def filtered_and_gram(n_patch, vectors, blocks, listed, live):
    tiles, _, width = vectors.shape
    nnz = blocks.shape[1]
    planes = n_patch // RING
    chunk = 4 * TILE // planes + 1
    part = width // SPLIT
    any_space = pl.BlockSpec(memory_space=pl.ANY)
    hbm = pl.BlockSpec(memory_space=pltpu.HBM)
    smem = pl.BlockSpec(memory_space=pltpu.SMEM)
    dma = pltpu.SemaphoreType.DMA
    side = [[pltpu.VMEM((3 * HALO, TILE, part), BF16) for _ in range(SPLIT)] for _ in range(STEPS)]
    return pl.pallas_call(
        functools.partial(filter_kernel, n_patch),
        out_shape=(
            jax.ShapeDtypeStruct((tiles, TILE, width), BF16),
            jax.ShapeDtypeStruct((tiles, TILE, width), BF16),
            jax.ShapeDtypeStruct((2, planes, chunk, TILE), F32),
        ),
        in_specs=[hbm, smem, hbm, hbm],
        out_specs=(any_space, any_space, any_space),
        scratch_shapes=[
            pltpu.SMEM((nnz, tiles), jnp.int32),
            pltpu.VMEM((tiles, TILE, width), BF16),
            pltpu.VMEM((tiles, nnz, TILE, TILE), BF16),
            [pltpu.VMEM((tiles, TILE, width), BF16) for _ in range(STEPS + 1)],
            side,
            side,
            pltpu.VMEM((tiles, TILE, width), BF16),
            pltpu.VMEM((width, 2 * width), F32),
            pltpu.VMEM((planes, chunk, TILE), F32),
            pltpu.VMEM((planes, chunk, TILE), F32),
            pltpu.VMEM((RING, chunk, TILE), F32),
            pltpu.VMEM((chunk, TILE), F32),
            dma((6,)),
            dma((tiles // HALO,)),
            dma((SPLIT, 2, PIECES)),
            dma((2, SPLIT, 2, PIECES)),
            dma((planes,)),
            dma((planes,)),
            dma((2 * STEPS - 1 + 2 * SPLIT,)),
            dma((planes - 1,)),
            dma((planes - 1,)),
            dma((planes - 1,)),
            dma((RING - 1,)),
            dma((RING - 1,)),
        ],
        compiler_params=pltpu.CompilerParams(
            collective_id=0, has_side_effects=True, vmem_limit_bytes=48 * 2**20
        ),
        name="filter_gram",
    )(listed, live, vectors, blocks)


def rotate_kernel(
    rows_total, gram, own_hbm, par_hbm, out_hbm, full, xh, xl, sh, sl, zmat, zh, zl, both_cores, out, in_sem, out_sem
):
    _, tiles, _, width = both_cores.shape
    size = 2 * width
    core = lax.axis_index("cols")
    loads = [
        pltpu.make_async_copy(own_hbm, both_cores.at[core], in_sem.at[0]),
        pltpu.make_async_copy(par_hbm, both_cores.at[1 - core], in_sem.at[1]),
    ]
    for copy in loads:
        copy.start()

    row = lax.broadcasted_iota(jnp.int32, (TILE, TILE), 0)
    lane = lax.broadcasted_iota(jnp.int32, (TILE, TILE), 1)
    per = gram.shape[1] // 4

    def piece(c, i):
        return gram[c, i * per : (i + 1) * per, : TILE // per, :].reshape(TILE, TILE)

    blocks = {}
    for c in range(2):
        mixed, line = piece(c, 0), jnp.sum(gram[c, :, TILE // per :, :], axis=0)
        flipped = mixed.T
        blocks[2 * c, 2 * c] = jnp.where(row <= lane, mixed, flipped)
        blocks[2 * c + 1, 2 * c + 1] = jnp.where(row > lane, mixed, jnp.where(row < lane, flipped, line))
        blocks[2 * c, 2 * c + 1] = piece(c, 1)
    blocks[0, 2], blocks[1, 3] = piece(0, 2), piece(0, 3)
    blocks[2, 1], blocks[3, 0] = piece(1, 2), piece(1, 3)
    total = sum((1.0 if i == j else 2.0) * jnp.sum(v * v, axis=0, keepdims=True) for (i, j), v in blocks.items())
    norm = jnp.sqrt(jnp.sum(total))
    inv = 1.0 / norm

    def put(i, j, value):
        full[i * TILE : (i + 1) * TILE, j * TILE : (j + 1) * TILE] = value

    for (i, j), value in blocks.items():
        value = value * inv
        if i <= j:
            put(i, j, value)
        if i > j or (i, j) in ((0, 1), (2, 3)):
            put(j, i, value.T)

    def split(value):
        high = value.astype(BF16)
        return high, (value - high.astype(F32)).astype(BF16)

    halves = [slice(i * width, (i + 1) * width) for i in range(2)]
    upper = ((0, 0), (0, 1), (1, 1))

    def keep(high, low, i, j, value):
        h, l = split(value)
        high[halves[i], halves[j]] = h
        low[halves[i], halves[j]] = l
        if i != j:
            high[halves[j], halves[i]] = h.T
            low[halves[j], halves[i]] = l.T

    for i, j in upper:
        keep(xh, xl, i, j, full[halves[i], halves[j]])
    mine = pl.ds(pl.multiple_of(core * width, width), width)
    eye = (
        lax.broadcasted_iota(jnp.int32, (size, width), 0)
        == lax.broadcasted_iota(jnp.int32, (size, width), 1) + core * width
    )
    z = jnp.where(eye, 1.5, 0.0) - 0.5 * (xh[:, mine].astype(F32) + xl[:, mine].astype(F32))
    zmat[...] = z
    zh[...], zl[...] = split(z)

    def times(count, ah, al, bh, bl, lanes):
        dot = functools.partial(jnp.dot, preferred_element_type=F32)
        high = ah[:count, :]
        both = dot(jnp.concatenate([high, al[:count, :]], axis=0), bh[:, lanes])
        return both[:count] + (both[count:] + dot(high, bl[:, lanes]))

    def square():
        for j in (1, 0):
            s = times((j + 1) * width, xh, xl, xh, xl, halves[j])
            rows = slice(0, (j + 1) * width)
            full[rows, halves[j]] = 2.25 * full[rows, halves[j]] - 1.5 * s
            for i in range(j + 1):
                keep(sh, sl, i, j, s[halves[i]])

    def cube():
        for j in (1, 0):
            rows = slice(0, (j + 1) * width)
            p = times((j + 1) * width, xh, xl, sh, sl, halves[j])
            full[rows, halves[j]] = full[rows, halves[j]] + 0.25 * p
        for i, j in upper:
            keep(xh, xl, i, j, full[halves[i], halves[j]])

    def turned():
        return 1.5 * zmat[...] - 0.5 * times(size, xh, xl, zh, zl, slice(None))

    def turn():
        zmat[...] = turned()
        zh[...], zl[...] = split(zmat[...])

    square()
    cube()

    def both(i, carry):
        square()
        turn()
        cube()
        return carry

    lax.fori_loop(1, ITERS - 1, both, 0)
    zh[...] = turned().astype(BF16)
    factor = jnp.sqrt(rows_total / norm)
    for copy in loads:
        copy.wait()
    group = GROUP
    stores = []

    def product(i):
        at = pl.ds(i * group, group)
        rows = [both_cores[c, at].reshape(group * TILE, width) for c in range(2)]
        return jnp.dot(jnp.concatenate(rows, axis=1), zh[...], preferred_element_type=F32)

    def finish(i, value):
        at = pl.ds(i * group, group)
        out[at] = (value * factor).astype(BF16).reshape(group, TILE, width)
        stores.append(pltpu.make_async_copy(out.at[at], out_hbm.at[at], out_sem.at[i]))
        stores[-1].start()

    value = product(0)
    for i in range(1, tiles // group):
        following = product(i)
        finish(i - 1, value)
        value = following
    finish(tiles // group - 1, value)
    for copy in stores:
        copy.wait()


def rotated(rows_total, gram, own, par):
    tiles, _, width = own.shape
    size = 2 * width
    any_space = pl.BlockSpec(memory_space=pl.ANY)
    vmem = pl.BlockSpec(memory_space=pltpu.VMEM)
    dma = pltpu.SemaphoreType.DMA
    return pl.pallas_call(
        functools.partial(rotate_kernel, rows_total),
        out_shape=jax.ShapeDtypeStruct(own.shape, BF16),
        in_specs=[vmem, any_space, any_space],
        out_specs=any_space,
        scratch_shapes=[
            pltpu.VMEM((size, size), F32),
            pltpu.VMEM((size, size), BF16),
            pltpu.VMEM((size, size), BF16),
            pltpu.VMEM((size, size), BF16),
            pltpu.VMEM((size, size), BF16),
            pltpu.VMEM((size, width), F32),
            pltpu.VMEM((size, width), BF16),
            pltpu.VMEM((size, width), BF16),
            pltpu.VMEM((2, tiles, TILE, width), BF16),
            pltpu.VMEM((tiles, TILE, width), BF16),
            dma((2,)),
            dma((tiles // GROUP,)),
        ],
        compiler_params=pltpu.CompilerParams(vmem_limit_bytes=48 * 2**20),
        name="rotate",
    )(gram, own, par)


def on_device(vectors, blocks, tile_cols, live_tiles):
    tiles, width = blocks.shape[0], vectors.shape[1]
    n_patch = lax.axis_size("patch")
    own, par, gram = filtered_and_gram(
        n_patch, vectors.reshape(tiles, TILE, width), blocks,
        pltpu.with_memory_space_constraint(tile_cols.T, pltpu.HBM), live_tiles,
    )
    result = rotated(n_patch * tiles * TILE, gram, own, par)
    return result.reshape(tiles * TILE, width)


def solution(mesh):
    in_specs = (P("patch", "cols"), P("patch", None, None, None), P("patch", None), P("patch"))
    out_specs = P("patch", "cols")
    return jax.shard_map(
        on_device, mesh=mesh, in_specs=in_specs, out_specs=out_specs, check_vma=False
    )
```

```python
import functools

import jax
import jax.numpy as jnp
from jax import lax
from jax.experimental import pallas as pl
from jax.experimental.pallas import tpu as pltpu
from jax.sharding import PartitionSpec as P

MESH = pl.DeviceIdType.MESH
F32, BF16 = jnp.float32, jnp.bfloat16
TILE = 128
HALO = 4
STEPS = 3
ITERS = 8
RING = 4
GROUP = 8
PIECES = 1
SPLIT = 2


def tdot(a, b):
    return lax.dot_general(a, b, (((0,), (0,)), ((), ())), preferred_element_type=F32)


def pack_gram(own, other, first, pay):
    row = lax.broadcasted_iota(jnp.int32, (TILE, TILE), 0)
    lane = lax.broadcasted_iota(jnp.int32, (TILE, TILE), 1)
    last = own[TILE:, TILE:]
    blocks = (
        jnp.where(row <= lane, own[:TILE, :TILE], last),
        own[:TILE, TILE:],
        jnp.where(first, other[:TILE, :TILE], other[:TILE, TILE:]),
        jnp.where(first, other[TILE:, TILE:], other[TILE:, :TILE]),
    )
    chunks = pay.shape[0]
    rows = 4 * TILE // chunks
    pay[:, :rows, :] = jnp.concatenate(blocks, axis=0).reshape(chunks, rows, TILE)
    line = jnp.sum(jnp.where(row == lane, last, 0.0), axis=0, keepdims=True)
    per = TILE // chunks
    for q in range(chunks):
        pay[q, rows:, :] = jnp.where(lane[:1] // per == q, line, 0.0)


def filter_kernel(
    n_patch, cols_hbm, live, vec, blk_hbm, own_out, par_out, gram_out,
    cols, raw, blk, ys, los, his, par, acc, pay, rsb, zb, tot,
    in_sem, blk_sem, halo_send, halo_recv, core_send, core_recv, swap_recv,
    plane_send, rs_recv, ag_recv, z_send, z_recv,
):
    tiles, width = raw.shape[0], raw.shape[2]
    part = width // SPLIT
    core, me = lax.axis_index("cols"), lax.axis_index("patch")
    planes = n_patch // RING
    plane, z = lax.div(me, RING), lax.rem(me, RING)
    px, py = lax.div(plane, RING), lax.rem(plane, RING)
    right, left = lax.rem(me + 1, n_patch), lax.rem(me + n_patch - 1, n_patch)

    def far(d):
        return sum(min(v, RING - v) for v in divmod(d, RING))

    offsets = sorted(range(1, planes), key=far, reverse=True)

    def plane_at(dx, dy):
        return lax.rem(px + dx, RING) * RING + lax.rem(py + dy, RING)

    peer_plane = {d: plane_at(*divmod(d, RING)) for d in offsets}
    source_plane = {d: plane_at(*((RING - v) % RING for v in divmod(d, RING))) for d in offsets}

    def plane_peer(d):
        return peer_plane[d] * RING + z

    def z_peer(d):
        return plane * RING + lax.rem(z + d, RING)

    def patch(index):
        return {"patch": index}

    def send(src, dst, ssem, rsem, target):
        return pltpu.make_async_remote_copy(
            src_ref=src, dst_ref=dst, send_sem=ssem, recv_sem=rsem,
            device_id=target, device_id_type=MESH,
        )

    edge = 2 * HALO
    mid = tiles - 2 * edge
    spans = ((0, HALO), (tiles - HALO, HALO), (HALO, HALO), (tiles - edge, HALO), (edge, mid))
    loads = [
        pltpu.make_async_copy(vec.at[pl.ds(s, n)], raw.at[pl.ds(s, n)], in_sem.at[i])
        for i, (s, n) in enumerate(spans)
    ]
    for copy in loads[:2]:
        copy.start()
    barrier = pltpu.get_barrier_semaphore()
    targets = [patch(right), patch(left), {"cols": 1 - core}]
    targets += [patch(plane_peer(d)) for d in offsets]
    targets += [patch(z_peer(d)) for d in range(1, RING)]
    for target in targets:
        pl.semaphore_signal(barrier, inc=1, device_id=target, device_id_type=MESH)
    list_load = pltpu.make_async_copy(cols_hbm, cols, in_sem.at[5])
    list_load.start()
    for copy in loads[2:]:
        copy.start()
    blk_loads = [
        pltpu.make_async_copy(blk_hbm.at[pl.ds(s, HALO)], blk.at[pl.ds(s, HALO)], blk_sem.at[i])
        for i, s in enumerate(range(0, tiles, HALO))
    ]
    for copy in blk_loads[1:] + blk_loads[:1]:
        copy.start()

    def weight(t):
        return (t < live[0]).astype(F32)

    def beside(k, t, value, h, lanes):
        if t < edge:
            los[k][h][t + HALO] = value[:, lanes]
        elif t >= tiles - edge:
            his[k][h][t - (tiles - edge)] = value[:, lanes]

    lanes_of = [slice(h * part, (h + 1) * part) for h in range(SPLIT)]

    def mask(t):
        value = (raw[t].astype(F32) * weight(t)).astype(BF16)
        ys[0][t] = value
        return value

    def mask_end(start):
        for t in range(start, start + HALO):
            value = mask(t)
            for h in range(SPLIT):
                beside(0, t, value, h, lanes_of[h])

    halos = {}
    half = HALO // PIECES

    def linked(up):
        return pl.when(me != n_patch - 1) if up else pl.when(me != 0)

    @pl.when(me == 0)
    def _():
        for k in range(STEPS):
            for h in range(SPLIT):
                los[k][h][:HALO] = jnp.zeros((HALO, TILE, part), BF16)

    @pl.when(me == n_patch - 1)
    def _():
        for k in range(STEPS):
            for h in range(SPLIT):
                his[k][h][2 * HALO :] = jnp.zeros((HALO, TILE, part), BF16)

    def launch(k, h, up, p):
        mine, theirs = (his, los) if up else (los, his)
        copy = send(
            mine[k][h].at[pl.ds(HALO + p * half, half)],
            theirs[k][h].at[pl.ds((0 if up else 2 * HALO) + p * half, half)],
            halo_send.at[h, int(up), p], halo_recv.at[k % 2, h, int(up), p], patch(right if up else left),
        )
        if k > 0:
            linked(up)(halos[k - 1, h, up, p].wait_send)
        linked(up)(copy.start)
        halos[k, h, up, p] = copy

    loads[0].wait()
    mask_end(0)
    loads[1].wait()
    mask_end(tiles - HALO)
    pl.semaphore_wait(barrier, len(targets))
    for h in range(SPLIT):
        for up in (True, False):
            for p in range(PIECES):
                launch(0, h, up, p)
    loads[2].wait()
    mask_end(HALO)
    loads[3].wait()
    mask_end(tiles - edge)
    loads[4].wait()

    def mask_mid(i, _):
        for j in range(HALO):
            mask(edge + i * HALO + j)
        return 0

    lax.fori_loop(0, mid // HALO, mask_mid, 0)

    def product(k, t, source, base, lanes):
        shift = me * tiles + base
        lhs = jnp.concatenate([blk[t, n] for n in range(blk.shape[1])], axis=1)
        slots = [jnp.clip(cols[n, t] - shift, 0, source.shape[0] - 1) for n in range(blk.shape[1])]
        rhs = jnp.concatenate([source[slot] for slot in slots], axis=0)
        total = jnp.dot(lhs, rhs, preferred_element_type=F32)
        if k > 1:
            total = 2.0 * total - ys[k - 2][t, :, lanes].astype(F32)
        return (total * weight(t)).astype(BF16)

    def inner(k, start, count, loading=False):
        def body(i, _):
            first = start + i * HALO
            if loading:
                rows = pl.ds(first, HALO)
                pltpu.make_async_copy(blk_hbm.at[rows], blk.at[rows], blk_sem.at[lax.div(first, HALO)]).wait()
            for j in range(HALO):
                t = first + j
                ys[k][t] = product(k, t, ys[k - 1], 0, slice(None))
            return 0

        lax.fori_loop(0, count // HALO, body, 0)

    swaps = []

    def swap(start, count, lanes):
        i = len(swaps)
        copy = send(
            ys[STEPS].at[pl.ds(start, count), :, lanes], par.at[pl.ds(start, count), :, lanes],
            core_send.at[i], swap_recv.at[i], {"cols": 1 - core},
        )
        copy.start()
        swaps.append(copy)

    every = slice(0, width)

    def copy_ends(k, first):
        for t in range(first, first + HALO):
            for h in range(SPLIT):
                beside(k, t, ys[k][t], h, lanes_of[h])

    def outer(k, h):
        for up in ((False, True) if k % 2 else (True, False)):
            side, slot = (his, tiles - edge) if up else (los, -HALO)
            first = tiles - HALO if up else 0
            for p in range(PIECES):
                linked(up)(halos[k - 1, h, not up, p].wait_recv)
            for p in range(PIECES):
                for t in range(first + p * half, first + (p + 1) * half):
                    value = product(k, t, side[k - 1][h], slot, lanes_of[h])
                    ys[k][t, :, lanes_of[h]] = value
                    if k < STEPS:
                        beside(k, t, value, h, slice(None))
                if k < STEPS:
                    launch(k, h, up, p)
            if k == STEPS:
                swap(first, HALO, lanes_of[h])

    list_load.wait()
    inner(1, HALO, tiles - 2 * HALO, loading=True)
    for copy in (blk_loads[0], blk_loads[-1]):
        copy.wait()
    copy_ends(1, HALO)
    copy_ends(1, tiles - edge)
    inner(2, 2 * HALO, tiles - 4 * HALO)

    def gram(start, count, step):
        def body(i, _):
            rows = pl.ds(start + i * step, step)
            mine = ys[STEPS][rows].reshape(step * TILE, width)
            other = par[rows].reshape(step * TILE, width)
            acc[:, :width] += tdot(mine, mine)
            acc[:, width:] += tdot(mine, other)
            return 0

        lax.fori_loop(0, count // step, body, 0)

    acc[...] = jnp.zeros_like(acc)
    for k in range(1, STEPS + 1):
        for h in range(SPLIT):
            outer(k, h)
        if k == 1:
            for start in (HALO, tiles - edge):
                inner(2, start, HALO)
                copy_ends(2, start)
            inner(STEPS, HALO * STEPS, tiles - 2 * HALO * STEPS)
            swap(HALO * STEPS, tiles - 2 * HALO * STEPS, every)
        if k == 2:
            for start in (2 * HALO, tiles - 3 * HALO, HALO, tiles - edge):
                inner(STEPS, start, HALO)
                swap(start, HALO, every)
        if k == STEPS - 1:
            early = len(swaps)
            for copy in swaps:
                copy.wait_recv()
            gram(HALO, tiles - 2 * HALO, edge)
    own_copy = pltpu.make_async_copy(ys[STEPS], own_out, in_sem.at[0])
    own_copy.start()

    def ends(ref):
        rows = [ref[pl.ds(s, HALO)].reshape(HALO * TILE, width) for s in (0, tiles - HALO)]
        return jnp.concatenate(rows, axis=0)

    mine = ends(ys[STEPS])
    acc[:, :width] += tdot(mine, mine)
    for copy in swaps[early:]:
        copy.wait_recv()
    par_copy = pltpu.make_async_copy(par, par_out, in_sem.at[1])
    par_copy.start()
    acc[:, width:] += tdot(ends(ys[STEPS]), ends(par))
    pack_gram(acc[:, :width], acc[:, width:], core == 0, pay)

    scatter = []
    for d in offsets:
        copy = send(pay.at[peer_plane[d]], rsb.at[d], plane_send.at[d - 1], rs_recv.at[d - 1], patch(plane_peer(d)))
        copy.start()
        scatter.append(copy)
    total = pay[plane]
    for d, copy in zip(offsets[::-1], scatter[::-1]):
        copy.wait_recv()
        total = total + rsb[d]
    zb[z] = total
    along = []
    for d in range(1, RING):
        copy = send(zb.at[z], zb.at[z], z_send.at[d - 1], z_recv.at[d - 1], patch(z_peer(d)))
        copy.start()
        along.append(copy)
    for (k, h, up, p), copy in halos.items():
        if k == STEPS - 1:
            linked(up)(copy.wait_send)
    for copy in swaps + scatter:
        copy.wait_send()
    own_copy.wait()
    par_copy.wait()
    for copy in along:
        copy.wait_recv()
    total = zb[0]
    for d in range(1, RING):
        total = total + zb[d]
    for copy in along:
        copy.wait_send()
    tot[...] = total
    gather = []
    for d in offsets:
        copy = send(tot, gram_out.at[core, plane], plane_send.at[d - 1], ag_recv.at[d - 1], patch(plane_peer(d)))
        copy.start()
        gather.append(copy)
    across = []

    def cross(d, src, at):
        copy = send(src, gram_out.at[core, at], core_send.at[d], core_recv.at[d], {"cols": 1 - core})
        copy.start()
        across.append(copy)

    cross(0, tot, plane)
    gram_copy = pltpu.make_async_copy(tot, gram_out.at[core, plane], in_sem.at[2])
    gram_copy.start()
    for d, copy in zip(offsets[::-1], gather[::-1]):
        copy.wait_recv()
        cross(d, gram_out.at[core, source_plane[d]], source_plane[d])
    for copy in across:
        copy.wait_recv()
    for copy in gather + across:
        copy.wait_send()
    gram_copy.wait()


def filtered_and_gram(n_patch, vectors, blocks, listed, live):
    tiles, _, width = vectors.shape
    nnz = blocks.shape[1]
    planes = n_patch // RING
    chunk = 4 * TILE // planes + 1
    part = width // SPLIT
    any_space = pl.BlockSpec(memory_space=pl.ANY)
    hbm = pl.BlockSpec(memory_space=pltpu.HBM)
    smem = pl.BlockSpec(memory_space=pltpu.SMEM)
    dma = pltpu.SemaphoreType.DMA
    side = [[pltpu.VMEM((3 * HALO, TILE, part), BF16) for _ in range(SPLIT)] for _ in range(STEPS)]
    return pl.pallas_call(
        functools.partial(filter_kernel, n_patch),
        out_shape=(
            jax.ShapeDtypeStruct((tiles, TILE, width), BF16),
            jax.ShapeDtypeStruct((tiles, TILE, width), BF16),
            jax.ShapeDtypeStruct((2, planes, chunk, TILE), F32),
        ),
        in_specs=[hbm, smem, hbm, hbm],
        out_specs=(any_space, any_space, any_space),
        scratch_shapes=[
            pltpu.SMEM((nnz, tiles), jnp.int32),
            pltpu.VMEM((tiles, TILE, width), BF16),
            pltpu.VMEM((tiles, nnz, TILE, TILE), BF16),
            [pltpu.VMEM((tiles, TILE, width), BF16) for _ in range(STEPS + 1)],
            side,
            side,
            pltpu.VMEM((tiles, TILE, width), BF16),
            pltpu.VMEM((width, 2 * width), F32),
            pltpu.VMEM((planes, chunk, TILE), F32),
            pltpu.VMEM((planes, chunk, TILE), F32),
            pltpu.VMEM((RING, chunk, TILE), F32),
            pltpu.VMEM((chunk, TILE), F32),
            dma((6,)),
            dma((tiles // HALO,)),
            dma((SPLIT, 2, PIECES)),
            dma((2, SPLIT, 2, PIECES)),
            dma((planes,)),
            dma((planes,)),
            dma((2 * STEPS - 1 + 2 * SPLIT,)),
            dma((planes - 1,)),
            dma((planes - 1,)),
            dma((planes - 1,)),
            dma((RING - 1,)),
            dma((RING - 1,)),
        ],
        compiler_params=pltpu.CompilerParams(
            collective_id=0, has_side_effects=True, vmem_limit_bytes=48 * 2**20
        ),
        name="filter_gram",
    )(listed, live, vectors, blocks)


def rotate_kernel(
    rows_total, gram, own_hbm, par_hbm, out_hbm, full, xh, xl, sh, sl, zmat, zh, zl, both_cores, out, in_sem, out_sem
):
    _, tiles, _, width = both_cores.shape
    size = 2 * width
    core = lax.axis_index("cols")
    loads = [
        pltpu.make_async_copy(own_hbm, both_cores.at[core], in_sem.at[0]),
        pltpu.make_async_copy(par_hbm, both_cores.at[1 - core], in_sem.at[1]),
    ]
    for copy in loads:
        copy.start()

    row = lax.broadcasted_iota(jnp.int32, (TILE, TILE), 0)
    lane = lax.broadcasted_iota(jnp.int32, (TILE, TILE), 1)
    per = gram.shape[1] // 4

    def piece(c, i):
        return gram[c, i * per : (i + 1) * per, : TILE // per, :].reshape(TILE, TILE)

    blocks = {}
    for c in range(2):
        mixed, line = piece(c, 0), jnp.sum(gram[c, :, TILE // per :, :], axis=0)
        flipped = mixed.T
        blocks[2 * c, 2 * c] = jnp.where(row <= lane, mixed, flipped)
        blocks[2 * c + 1, 2 * c + 1] = jnp.where(row > lane, mixed, jnp.where(row < lane, flipped, line))
        blocks[2 * c, 2 * c + 1] = piece(c, 1)
    blocks[0, 2], blocks[1, 3] = piece(0, 2), piece(0, 3)
    blocks[2, 1], blocks[3, 0] = piece(1, 2), piece(1, 3)
    total = sum((1.0 if i == j else 2.0) * jnp.sum(v * v, axis=0, keepdims=True) for (i, j), v in blocks.items())
    norm = jnp.sqrt(jnp.sum(total))
    inv = 1.0 / norm

    def put(i, j, value):
        full[i * TILE : (i + 1) * TILE, j * TILE : (j + 1) * TILE] = value

    for (i, j), value in blocks.items():
        value = value * inv
        if i <= j:
            put(i, j, value)
        if i > j or (i, j) in ((0, 1), (2, 3)):
            put(j, i, value.T)

    def split(value):
        high = value.astype(BF16)
        return high, (value - high.astype(F32)).astype(BF16)

    halves = [slice(i * width, (i + 1) * width) for i in range(2)]
    upper = ((0, 0), (0, 1), (1, 1))

    def keep(high, low, i, j, value):
        h, l = split(value)
        high[halves[i], halves[j]] = h
        low[halves[i], halves[j]] = l
        if i != j:
            high[halves[j], halves[i]] = h.T
            low[halves[j], halves[i]] = l.T

    for i, j in upper:
        keep(xh, xl, i, j, full[halves[i], halves[j]])
    mine = pl.ds(pl.multiple_of(core * width, width), width)
    eye = (
        lax.broadcasted_iota(jnp.int32, (size, width), 0)
        == lax.broadcasted_iota(jnp.int32, (size, width), 1) + core * width
    )
    z = jnp.where(eye, 1.5, 0.0) - 0.5 * (xh[:, mine].astype(F32) + xl[:, mine].astype(F32))
    zmat[...] = z
    zh[...], zl[...] = split(z)

    def times(count, ah, al, bh, bl, lanes):
        dot = functools.partial(jnp.dot, preferred_element_type=F32)
        high = ah[:count, :]
        both = dot(jnp.concatenate([high, al[:count, :]], axis=0), bh[:, lanes])
        return both[:count] + (both[count:] + dot(high, bl[:, lanes]))

    def square():
        for j in (1, 0):
            s = times((j + 1) * width, xh, xl, xh, xl, halves[j])
            rows = slice(0, (j + 1) * width)
            full[rows, halves[j]] = 2.25 * full[rows, halves[j]] - 1.5 * s
            for i in range(j + 1):
                keep(sh, sl, i, j, s[halves[i]])

    def cube():
        for j in (1, 0):
            rows = slice(0, (j + 1) * width)
            p = times((j + 1) * width, xh, xl, sh, sl, halves[j])
            full[rows, halves[j]] = full[rows, halves[j]] + 0.25 * p
        for i, j in upper:
            keep(xh, xl, i, j, full[halves[i], halves[j]])

    def turned():
        return 1.5 * zmat[...] - 0.5 * times(size, xh, xl, zh, zl, slice(None))

    def turn():
        zmat[...] = turned()
        zh[...], zl[...] = split(zmat[...])

    square()
    cube()

    def both(i, carry):
        square()
        turn()
        cube()
        return carry

    lax.fori_loop(1, ITERS - 1, both, 0)
    zh[...] = turned().astype(BF16)
    factor = jnp.sqrt(rows_total / norm)
    for copy in loads:
        copy.wait()
    group = GROUP
    stores = []

    def product(i):
        at = pl.ds(i * group, group)
        rows = [both_cores[c, at].reshape(group * TILE, width) for c in range(2)]
        return jnp.dot(jnp.concatenate(rows, axis=1), zh[...], preferred_element_type=F32)

    def finish(i, value):
        at = pl.ds(i * group, group)
        out[at] = (value * factor).astype(BF16).reshape(group, TILE, width)
        stores.append(pltpu.make_async_copy(out.at[at], out_hbm.at[at], out_sem.at[i]))
        stores[-1].start()

    value = product(0)
    for i in range(1, tiles // group):
        following = product(i)
        finish(i - 1, value)
        value = following
    finish(tiles // group - 1, value)
    for copy in stores:
        copy.wait()


def rotated(rows_total, gram, own, par):
    tiles, _, width = own.shape
    size = 2 * width
    any_space = pl.BlockSpec(memory_space=pl.ANY)
    vmem = pl.BlockSpec(memory_space=pltpu.VMEM)
    dma = pltpu.SemaphoreType.DMA
    return pl.pallas_call(
        functools.partial(rotate_kernel, rows_total),
        out_shape=jax.ShapeDtypeStruct(own.shape, BF16),
        in_specs=[vmem, any_space, any_space],
        out_specs=any_space,
        scratch_shapes=[
            pltpu.VMEM((size, size), F32),
            pltpu.VMEM((size, size), BF16),
            pltpu.VMEM((size, size), BF16),
            pltpu.VMEM((size, size), BF16),
            pltpu.VMEM((size, size), BF16),
            pltpu.VMEM((size, width), F32),
            pltpu.VMEM((size, width), BF16),
            pltpu.VMEM((size, width), BF16),
            pltpu.VMEM((2, tiles, TILE, width), BF16),
            pltpu.VMEM((tiles, TILE, width), BF16),
            dma((2,)),
            dma((tiles // GROUP,)),
        ],
        compiler_params=pltpu.CompilerParams(
            vmem_limit_bytes=48 * 2**20
        ),
        name="rotate",
    )(gram, own, par)


def on_device(vectors, blocks, tile_cols, live_tiles):
    tiles, width = blocks.shape[0], vectors.shape[1]
    n_patch = lax.axis_size("patch")
    own, par, gram = filtered_and_gram(
        n_patch, vectors.reshape(tiles, TILE, width), blocks,
        pltpu.with_memory_space_constraint(tile_cols.T, pltpu.HBM), live_tiles,
    )
    result = rotated(n_patch * tiles * TILE, gram, own, par)
    return result.reshape(tiles * TILE, width)


def solution(mesh):
    in_specs = (P("patch", "cols"), P("patch", None, None, None), P("patch", None), P("patch"))
    out_specs = P("patch", "cols")
    return jax.shard_map(
        on_device, mesh=mesh, in_specs=in_specs, out_specs=out_specs, check_vma=False
    )
```
